512 devices in a mesh: space: 256 (over z, y, x), wt: 2 (over core).
Axes of the slice: x: 4, y: 8, z: 8, core: 2. Of those that a mesh axis runs over, the one named last changes fastest.
Arguments:
- features: bfloat16 [512, 8, 8, 8, 192], P(('space', 'wt')), may hold values from -6 to 6
- occupancy: int32 [512], P(('space', 'wt')), may hold values from 0 to 1, as said below
- neighbours: int32 [512, 27], P(('space', 'wt')), may hold values from -1 to 511, as said below
- kernel_one: bfloat16 [3, 3, 3, 48, 768], P(None, None, None, None, 'wt'), may hold values from -0.078125 to 0.078125
- kernel_two: bfloat16 [3, 3, 3, 48, 768], P(None, None, None, None, 'wt'), may hold values from -0.078125 to 0.078125
Outputs:
- block_out: float32 [512, 8, 8, 8, 192], P(('space', 'wt'))
The draws below stay inside these ranges and needn't reach their ends.
Inputs may be any that keep to these rules, and one draw needn't show every extreme that they name: `occupancy`: the first slot of every device's 1 slots is active; the others are active with probability three quarters. `neighbours`: entries are -1 or an active slot; for an active slot s, entry 13 is s itself, and every other entry lies among the slots of the same device, the previous or the next device in slot order (slots d * 1 to (d+1) - 1 belong to device d). Rows of inactive slots are all -1.
All inputs are finite; a program needn't handle non-finite values.
Results may differ from the reference program's by a relative error of at most 0.0018.
Values may be sent and summed in bfloat16 or wider, within the bound.
A program may use at most 64 MiB of HBM per device.

```python
import jax
import jax.numpy as jnp
from jax import lax

C = 192
BLK_DEV = 1
SLOTS = 512


def common_blocks(key):
    key_occ = jax.random.fold_in(key, 101)
    key_pick = jax.random.fold_in(key, 202)
    key_slot = jax.random.fold_in(key, 303)
    key_miss = jax.random.fold_in(key, 404)
    slot_ids = jnp.arange(SLOTS, dtype=jnp.int32)
    occupied = (jax.random.randint(key_occ, (SLOTS,), 0, 4) > 0) | (slot_ids % BLK_DEV == 0)
    device_ids = slot_ids // BLK_DEV
    step_dev = jax.random.randint(key_pick, (SLOTS, 27), -1, 2)
    inner = jax.random.randint(key_slot, (SLOTS, 27), 0, BLK_DEV)
    candidate = (device_ids[:, None] + step_dev) * BLK_DEV + inner
    inside = (candidate >= 0) & (candidate < SLOTS)
    safe = jnp.clip(candidate, 0, SLOTS - 1)
    keep = jax.random.randint(key_miss, (SLOTS, 27), 0, 5) > 0
    valid = inside & occupied[safe] & keep
    table = jnp.where(valid, safe, -1)
    table = table.at[:, 13].set(slot_ids)
    table = jnp.where(occupied[:, None], table, -1)
    return (occupied.astype(jnp.int32), table.astype(jnp.int32))


def draw_occupancy(key, part):
    return common_blocks(key)[0]


def draw_neighbours(key, part):
    return common_blocks(key)[1]


def block_scale(stream_key, extent, split, low, top_value):
    def one(dim, shards_of):
        draws = jax.random.uniform(jax.random.fold_in(jax.random.fold_in(stream_key, 6), dim), (shards_of,), jnp.float32, low / len(split), top_value / len(split))
        return jnp.repeat(jnp.exp(draws), extent[dim] // shards_of).reshape((-1,) + (1,) * (len(extent) - dim - 1))

    loudness = one(*split[0])
    for cut in split[1:]:
        loudness = loudness * one(*cut)
    return loudness


def normal_values(own_key, shape, scale, limit, shards=(), kind=jnp.bfloat16):
    values = scale * jax.random.normal(own_key, shape, jnp.float32)
    if shards:
        values = values * block_scale(own_key, shape, shards, -0.22, 0.18)
    return jnp.clip(values, -limit, limit).astype(kind)


def setup_inputs(seed: int = 0) -> dict:
    seeds = jax.random.split(jax.random.key(seed), 6)
    return {
        "features": normal_values(seeds[0], (SLOTS, 8, 8, 8, C), 1.0, 6.0, ((0, 512),)),
        "occupancy": draw_occupancy(jax.random.fold_in(seeds[5], 71), 0),
        "neighbours": draw_neighbours(jax.random.fold_in(seeds[5], 71), 0),
        "kernel_one": normal_values(seeds[3], (3, 3, 3, C // 4, 4 * C), (27 * C) ** -0.5, 0.078125, ((4, 2),)),
        "kernel_two": normal_values(seeds[4], (3, 3, 3, C // 4, 4 * C), (27 * C) ** -0.5, 0.078125, ((4, 2),)),
    }


def unpack_kernel(stored):
    quarter = stored.shape[3]
    width = stored.shape[4] // 4
    grouped = stored.reshape(3, 3, 3, quarter, 4, width)
    return jnp.transpose(grouped, (0, 1, 2, 4, 3, 5)).reshape(3, 3, 3, 4 * quarter, width)


def pad_blocks(source, index):
    ranges = ((7, 8), (0, 8), (0, 1))
    planes = []
    for first in range(3):
        rows = []
        for second in range(3):
            cols = []
            for third in range(3):
                tap = first * 9 + second * 3 + third
                which = index[:, tap]
                picked = jnp.take(source, jnp.maximum(which, 0).astype(jnp.int32), axis=0)
                lo_a, hi_a = ranges[first]
                lo_b, hi_b = ranges[second]
                lo_c, hi_c = ranges[third]
                piece = picked[:, lo_a:hi_a, lo_b:hi_b, lo_c:hi_c, :]
                valid = (which >= 0)[:, None, None, None, None]
                cols.append(jnp.where(valid, piece, jnp.zeros((), piece.dtype)))
            rows.append(jnp.concatenate(cols, axis=3))
        planes.append(jnp.concatenate(rows, axis=2))
    return jnp.concatenate(planes, axis=1)


def conv_taps(padded, kernel):
    return lax.conv_general_dilated(padded.astype(jnp.float32), kernel.astype(jnp.float32), (1, 1, 1), "VALID", dimension_numbers=("NDHWC", "DHWIO", "NDHWC"), precision=lax.Precision.HIGHEST)


def apply_layer(source, neighbours, kernel):
    groups = SLOTS // BLK_DEV

    def one_group(group):
        index = lax.dynamic_slice_in_dim(neighbours, (group * BLK_DEV).astype(jnp.int32), BLK_DEV, 0)
        return conv_taps(pad_blocks(source, index), kernel)

    result = lax.map(one_group, jnp.arange(groups, dtype=jnp.int32))
    return result.reshape(source.shape[0], 8, 8, 8, kernel.shape[4])


def reference(features, occupancy, neighbours, kernel_one, kernel_two):
    active = occupancy.astype(jnp.float32)[:, None, None, None, None]
    hidden = (jax.nn.relu(apply_layer(features, neighbours, unpack_kernel(kernel_one))) * active).astype(jnp.bfloat16)
    return jax.nn.relu(features.astype(jnp.float32) + apply_layer(hidden, neighbours, unpack_kernel(kernel_two))) * active
```

```python
import functools

import jax
import jax.numpy as jnp
from jax import lax
from jax.experimental import pallas as pl
from jax.experimental.pallas import tpu as pltpu
from jax.sharding import PartitionSpec as P

C = 192
MESH = pl.DeviceIdType.MESH
F32 = jnp.float32
BF16 = jnp.bfloat16


def kernel(
    total, feat, occ, nbr, wk1, wk2, out,
    fsrc, hsrc, wbuf1, wbuf2, wfull, cols, tab, occs,
    lsem, fsend, frecv, wsend, wrecv, hsend, hrecv,
):
    space = lax.axis_index("space")
    core = lax.axis_index("wt")
    me = space * 2 + core
    after = me + 1
    before = me - 1
    has_after = after < total
    has_before = before >= 0
    after_id = (after // 2, after % 2)
    before_id = (lax.max(before, 0) // 2, lax.max(before, 0) % 2)
    mate_id = (space, 1 - core)

    local = [
        pltpu.make_async_copy(feat, fsrc.at[2], lsem.at[0]),
        pltpu.make_async_copy(nbr, tab, lsem.at[1]),
        pltpu.make_async_copy(occ, occs, lsem.at[2]),
        pltpu.make_async_copy(wk1, wbuf1.at[core], lsem.at[3]),
        pltpu.make_async_copy(wk2, wbuf2.at[core], lsem.at[4]),
    ]
    for copy in local:
        copy.start()

    barrier = pltpu.get_barrier_semaphore()

    @pl.when(has_after)
    def _():
        pl.semaphore_signal(barrier, inc=1, device_id=after_id, device_id_type=MESH)

    @pl.when(has_before)
    def _():
        pl.semaphore_signal(barrier, inc=1, device_id=before_id, device_id_type=MESH)

    fsrc[0] = jnp.zeros((8, 64, C), BF16)
    hsrc[0] = jnp.zeros((8, 64, C), BF16)

    pl.semaphore_wait(barrier, has_after.astype(jnp.int32) + has_before.astype(jnp.int32))

    def to_after(source, target, sems, recvs, i):
        return pltpu.make_async_remote_copy(
            src_ref=source, dst_ref=target, send_sem=sems.at[0, i], recv_sem=recvs.at[0, i],
            device_id=after_id, device_id_type=MESH)

    def to_before(source, target, sems, recvs, i):
        return pltpu.make_async_remote_copy(
            src_ref=source, dst_ref=target, send_sem=sems.at[1, i], recv_sem=recvs.at[1, i],
            device_id=before_id, device_id_type=MESH)

    fa = to_after(feat, fsrc.at[1], fsend, frecv, 0)
    fb = to_before(feat, fsrc.at[3], fsend, frecv, 0)
    pl.when(has_after)(fa.start)
    pl.when(has_before)(fb.start)

    wcopies = []
    for layer, (wk, wbuf) in enumerate(((wk1, wbuf1), (wk2, wbuf2))):
        for i in range(3):
            wcopies.append(pltpu.make_async_remote_copy(
                src_ref=wk.at[i], dst_ref=wbuf.at[core, i],
                send_sem=wsend.at[layer, i], recv_sem=wrecv.at[layer, i],
                device_id=mate_id, device_id_type=MESH))
    for copy in wcopies:
        copy.start()

    local[1].wait()
    local[2].wait()
    where = [None] * 27
    for t in range(27):
        n = tab[0, t]
        where[t] = jnp.where(n >= 0, jnp.clip(n - me + 2, 1, 3), 0)
    active = occs[0].astype(F32)

    zi = lax.broadcasted_iota(jnp.int32, (80, C), 0) % 8

    def build(src):
        def plane(X, a, xp):
            def line(c):
                def at(b):
                    t = 9 * (a + 1) + 3 * (b + 1) + (c + 1)
                    return 2 if t == 13 else where[t]
                return jnp.concatenate([
                    src[at(-1), xp, 56:64, :].astype(F32),
                    src[at(0), xp].astype(F32),
                    src[at(1), xp, 0:8, :].astype(F32),
                ], axis=0)
            left, mid, right = line(-1), line(0), line(1)
            lo = jnp.where(zi == 7, left, mid).reshape(10, 8, C)
            hi = jnp.where(zi == 0, right, mid).reshape(10, 8, C)
            shifted = (
                pltpu.roll(lo, 1, 1).reshape(80, C),
                mid,
                pltpu.roll(hi, 7, 1).reshape(80, C),
            )
            for k in range(3):
                for j in range(3):
                    cols[X, :, (3 * j + k) * C:(3 * j + k + 1) * C] = (
                        shifted[k][8 * j:8 * j + 64].astype(BF16))

        plane(0, -1, 7)
        plane(9, 1, 0)

        @pl.loop(0, 8)
        def _(x):
            plane(x + 1, 0, x)

    def unpack(wbuf, h, i):
        for jk in range(9):
            tile = wbuf[h, i, jk // 3, jk % 3]
            base = jk * C + h * 96
            base = pl.multiple_of(base, 16)
            wfull[i, pl.ds(base, 48), :] = tile[:, 0:C]
            wfull[i, pl.ds(pl.multiple_of(base + 48, 16), 48), :] = tile[:, C:2 * C]

    def conv_half(m):
        acc = None
        for i in range(3):
            lhs = cols[4 * m + i:4 * m + i + 4].reshape(256, 9 * C)
            d = jnp.dot(lhs, wfull[i], preferred_element_type=F32)
            acc = d if acc is None else acc + d
        return acc

    mate = 1 - core
    local[3].wait()
    for i in range(3):
        unpack(wbuf1, core, i)
    for i in range(3):
        wcopies[i].wait_recv()
        unpack(wbuf1, mate, i)

    local[0].wait()
    pl.when(has_before)(fa.wait_recv)
    pl.when(has_after)(fb.wait_recv)
    build(fsrc)
    ha = []
    hb = []
    for m in range(2):
        acc = conv_half(m)
        h = (jnp.maximum(acc, 0.0) * active).astype(BF16)
        hsrc[2, 4 * m:4 * m + 4] = h.reshape(4, 64, C)
        part = pl.ds(4 * m, 4)
        ha.append(to_after(hsrc.at[2, part], hsrc.at[1, part], hsend, hrecv, m))
        hb.append(to_before(hsrc.at[2, part], hsrc.at[3, part], hsend, hrecv, m))
        pl.when(has_after)(ha[m].start)
        pl.when(has_before)(hb[m].start)

    local[4].wait()
    for i in range(3):
        unpack(wbuf2, core, i)
    for i in range(3):
        wcopies[3 + i].wait_recv()
        unpack(wbuf2, mate, i)
    for m in range(2):
        pl.when(has_before)(ha[m].wait_recv)
        pl.when(has_after)(hb[m].wait_recv)
    build(hsrc)
    for m in range(2):
        acc = conv_half(m)
        res = fsrc[2, 4 * m:4 * m + 4].reshape(256, C).astype(F32)
        o = jnp.maximum(res + acc, 0.0) * active
        out[4 * m:4 * m + 4] = o.reshape(4, 64, C)

    for copy in wcopies:
        copy.wait_send()
    pl.when(has_after)(fa.wait_send)
    pl.when(has_before)(fb.wait_send)
    for m in range(2):
        pl.when(has_after)(ha[m].wait_send)
        pl.when(has_before)(hb[m].wait_send)


def body(features, occupancy, neighbours, kernel_one, kernel_two):
    total = lax.axis_size("space") * lax.axis_size("wt")
    hbm = pl.BlockSpec(memory_space=pl.ANY)
    y = pl.pallas_call(
        functools.partial(kernel, total),
        out_shape=jax.ShapeDtypeStruct((8, 64, C), F32),
        in_specs=[hbm] * 5,
        out_specs=pl.BlockSpec(memory_space=pltpu.VMEM),
        scratch_shapes=[
            pltpu.VMEM((4, 8, 64, C), BF16),
            pltpu.VMEM((4, 8, 64, C), BF16),
            pltpu.VMEM((2, 3, 3, 3, 48, 2 * C), BF16),
            pltpu.VMEM((2, 3, 3, 3, 48, 2 * C), BF16),
            pltpu.VMEM((3, 9 * C, C), BF16),
            pltpu.VMEM((10, 64, 9 * C), BF16),
            pltpu.SMEM((1, 27), jnp.int32),
            pltpu.SMEM((1,), jnp.int32),
            pltpu.SemaphoreType.DMA((5,)),
            pltpu.SemaphoreType.DMA((2, 1)),
            pltpu.SemaphoreType.DMA((2, 1)),
            pltpu.SemaphoreType.DMA((2, 3)),
            pltpu.SemaphoreType.DMA((2, 3)),
            pltpu.SemaphoreType.DMA((2, 2)),
            pltpu.SemaphoreType.DMA((2, 2)),
        ],
        compiler_params=pltpu.CompilerParams(
            collective_id=0, has_side_effects=True, vmem_limit_bytes=60 * 1024 * 1024),
    )(features.reshape(8, 64, C), occupancy, neighbours, kernel_one, kernel_two)
    return y.reshape(1, 8, 8, 8, C)


def solution(mesh):
    return jax.shard_map(
        body,
        mesh=mesh,
        in_specs=(
            P(("space", "wt"), None, None, None, None),
            P(("space", "wt")),
            P(("space", "wt"), None),
            P(None, None, None, None, "wt"),
            P(None, None, None, None, "wt"),
        ),
        out_specs=P(("space", "wt"), None, None, None, None),
        check_vma=False,
    )
```

```python
import functools

import jax
import jax.numpy as jnp
from jax import lax
from jax.experimental import pallas as pl
from jax.experimental.pallas import tpu as pltpu
from jax.sharding import PartitionSpec as P

C = 192
MESH = pl.DeviceIdType.MESH
F32 = jnp.float32
BF16 = jnp.bfloat16
FACES = ((-1, 0, 0), (1, 0, 0), (0, -1, 0), (0, 1, 0), (0, 0, -1), (0, 0, 1))


def columns(dst, low, mid, high):
    row = lax.broadcasted_iota(jnp.int32, (80, C), 0) % 8
    lo = jnp.where(row == 7, low, mid).reshape(10, 8, C)
    hi = jnp.where(row == 0, high, mid).reshape(10, 8, C)
    shifted = (pltpu.roll(lo, 1, 1).reshape(80, C), mid, pltpu.roll(hi, 7, 1).reshape(80, C))
    for inner in range(3):
        for outer in range(3):
            at = (3 * outer + inner) * C
            dst[:, at:at + C] = shifted[inner][8 * outer:8 * outer + 64].astype(BF16)


def framed(value):
    edge = jnp.zeros((8, C), F32)
    return jnp.concatenate([edge, value, edge], axis=0)


def own_columns(cols, src):
    @pl.loop(0, 8)
    def _(x):
        columns(cols.at[x + 1], 0.0, framed(src[x].astype(F32)), 0.0)


def own_conv(cols, weights, half):
    acc = None
    for i in range(3):
        lhs = cols[4 * half + i:4 * half + i + 4].reshape(256, 9 * C)
        d = jnp.dot(lhs, weights[i], preferred_element_type=F32)
        acc = d if acc is None else acc + d
    return acc


def face_columns(dst, surf, where):
    def at(a, b, c):
        return where[9 * (a + 1) + 3 * (b + 1) + (c + 1)]

    def face(source, axis, side):
        pair = surf[source, axis]
        return (pair[:, C:] if side < 0 else pair[:, :C]).astype(F32)

    for n, (a, b, c) in enumerate(FACES):
        if a:
            def line(v):
                return jnp.concatenate([
                    face(at(a, -1, v), 0, a)[56:64],
                    face(at(a, 0, v), 0, a),
                    face(at(a, 1, v), 0, a)[0:8],
                ], axis=0)
            columns(dst.at[n], line(-1), line(0), line(1))
        elif b:
            columns(dst.at[n], *(framed(face(at(0, b, v), 1, b)) for v in (-1, 0, 1)))
        else:
            columns(dst.at[n], 0.0, framed(face(at(0, 0, c), 2, c)), 0.0)


def face_product(fcols, weights, n):
    a, b, c = FACES[n]
    if a:
        rhs = weights[a + 1]
    elif b:
        at = 3 * C * (b + 1)
        rhs = jnp.concatenate([weights[i, at:at + 3 * C] for i in range(3)], axis=0)
    else:
        rhs = jnp.concatenate(
            [weights[i, (3 * j + c + 1) * C:(3 * j + c + 2) * C] for i in range(3) for j in range(3)], axis=0)
    return jnp.dot(fcols[n], rhs, preferred_element_type=F32)


def put(acc, rows, value):
    acc[0, rows, :] = value[:, :128]
    acc[1, rows, 0:C - 128] = value[:, 128:]


def get(acc, rows):
    return jnp.concatenate([acc[0, rows, :], acc[1, rows, 0:C - 128]], axis=1)


def add_faces(acc, fcols, weights):
    for n, (a, b, c) in enumerate(FACES):
        d = face_product(fcols, weights, n)
        if a:
            rows = slice(0, 64) if a < 0 else slice(448, 512)
            put(acc, rows, get(acc, rows) + d)
        elif b:
            first = 0 if b < 0 else 56
            for x in range(8):
                rows = slice(64 * x + first, 64 * x + first + 8)
                put(acc, rows, get(acc, rows) + d[8 * x:8 * x + 8])
        else:
            rows = pl.ds(0 if c < 0 else 7, 64, stride=8)
            rest = jnp.concatenate([d[:, 128:], jnp.zeros((64, 256 - C), F32)], axis=1)
            for part, value in enumerate((d[:, :128], rest)):
                acc[part, rows, :] = acc[part, rows, :] + value


def pack_faces(dst, field, fix):
    def strided(first):
        rows = pl.ds(first, 64, stride=8)
        return jnp.concatenate([field[0, rows, :], field[1, rows, :][:, 0:C - 128]], axis=1)

    dst[0, :, :C] = fix(get(field, slice(0, 64)))
    dst[0, :, C:] = fix(get(field, slice(448, 512)))
    for side, first in enumerate((0, 56)):
        rows = jnp.concatenate(
            [get(field, slice(64 * x + first, 64 * x + first + 8)) for x in range(8)], axis=0)
        dst[1, :, side * C:(side + 1) * C] = fix(rows)
    dst[2, :, :C] = fix(strided(0))
    dst[2, :, C:] = fix(strided(7))


def exchange_kernel(
    total, feat, occ, nbr, wk1, wk2,
    hcols, w2, acc2, act,
    own, fsurf, hsurf, wbuf1, wbuf2, w1, cols, fcols, acc, tab, occs,
    lsem, fsend, frecv, wsend, wrecv, hsend, hrecv,
):
    space = lax.axis_index("space")
    core = lax.axis_index("wt")
    mate = 1 - core
    me = space * 2 + core
    after = me + 1
    before = me - 1
    has_after = after < total
    has_before = before >= 0
    after_id = (after // 2, after % 2)
    before_id = (lax.max(before, 0) // 2, lax.max(before, 0) % 2)

    barrier = pltpu.get_barrier_semaphore()

    @pl.when(has_after)
    def _():
        pl.semaphore_signal(barrier, inc=1, device_id=after_id, device_id_type=MESH)

    @pl.when(has_before)
    def _():
        pl.semaphore_signal(barrier, inc=1, device_id=before_id, device_id_type=MESH)

    local = [
        pltpu.make_async_copy(feat, own, lsem.at[0]),
        pltpu.make_async_copy(nbr, tab, lsem.at[1]),
        pltpu.make_async_copy(occ, occs, lsem.at[2]),
        pltpu.make_async_copy(wk1, wbuf1.at[core], lsem.at[3]),
        pltpu.make_async_copy(wk2, wbuf2.at[core], lsem.at[4]),
    ]
    for copy in local:
        copy.start()

    fsurf[0] = jnp.zeros((3, 64, 2 * C), BF16)
    hsurf[0] = jnp.zeros((3, 64, 2 * C), BF16)
    cols[0] = jnp.zeros((64, 9 * C), BF16)
    cols[9] = jnp.zeros((64, 9 * C), BF16)

    local[0].wait()
    for x in range(8):
        put(acc, slice(64 * x, 64 * x + 64), own[x].astype(F32))
    pack_faces(fsurf.at[2], acc, lambda v: v.astype(BF16))

    pl.semaphore_wait(barrier, has_after.astype(jnp.int32) + has_before.astype(jnp.int32))

    def sends(surf, sems, recvs):
        ahead = pltpu.make_async_remote_copy(
            src_ref=surf.at[2], dst_ref=surf.at[1], send_sem=sems.at[0], recv_sem=recvs.at[0],
            device_id=after_id, device_id_type=MESH)
        back = pltpu.make_async_remote_copy(
            src_ref=surf.at[2], dst_ref=surf.at[3], send_sem=sems.at[1], recv_sem=recvs.at[1],
            device_id=before_id, device_id_type=MESH)
        return ahead, back

    fa, fb = sends(fsurf, fsend, frecv)
    pl.when(has_after)(fa.start)
    pl.when(has_before)(fb.start)
    wcopies = [
        pltpu.make_async_remote_copy(
            src_ref=wk, dst_ref=wbuf.at[core], send_sem=wsend.at[n], recv_sem=wrecv.at[n],
            device_id=(space, mate), device_id_type=MESH)
        for n, (wk, wbuf) in enumerate(((wk1, wbuf1), (wk2, wbuf2)))
    ]
    for copy in wcopies:
        copy.start()

    local[1].wait()
    local[2].wait()
    where = []
    for t in range(27):
        n = tab[0, t]
        where.append(jnp.where(n >= 0, jnp.clip(n - me + 2, 1, 3), 0))
    active = occs[0].astype(F32)

    def unpack(wbuf, weights, h):
        base = pl.multiple_of(h * 96, 16)

        @pl.loop(0, 3)
        def _(i):
            for jk in range(9):
                tile = wbuf[h, i, jk // 3, jk % 3]
                weights[i, pl.ds(base + jk * C, 48), :] = tile[:, 0:C]
                weights[i, pl.ds(base + jk * C + 48, 48), :] = tile[:, C:2 * C]

    own_columns(cols, own)
    local[3].wait()
    unpack(wbuf1, w1, core)
    wcopies[0].wait_recv()
    unpack(wbuf1, w1, mate)
    for half in range(2):
        put(acc, slice(256 * half, 256 * half + 256), own_conv(cols, w1, half))
    local[4].wait()
    unpack(wbuf2, w2, core)
    wcopies[1].wait_recv()
    unpack(wbuf2, w2, mate)

    pl.when(has_before)(fa.wait_recv)
    pl.when(has_after)(fb.wait_recv)
    face_columns(fcols, fsurf, where)
    add_faces(acc, fcols, w1)

    def hidden(v):
        return (jnp.maximum(v, 0.0) * active).astype(BF16)

    pack_faces(hsurf.at[2], acc, hidden)
    ha, hb = sends(hsurf, hsend, hrecv)
    pl.when(has_after)(ha.start)
    pl.when(has_before)(hb.start)

    @pl.loop(0, 8)
    def _(x):
        v = hidden(get(acc, pl.ds(pl.multiple_of(64 * x, 64), 64)))
        columns(cols.at[x + 1], 0.0, framed(v.astype(F32)), 0.0)

    for half in range(2):
        res = own[4 * half:4 * half + 4].reshape(256, C).astype(F32)
        put(acc2, slice(256 * half, 256 * half + 256), res + own_conv(cols, w2, half))
    act[...] = jnp.full((8, C), active, F32)

    for copy in wcopies:
        copy.wait_send()
    pl.when(has_after)(fa.wait_send)
    pl.when(has_before)(fb.wait_send)
    pl.when(has_before)(ha.wait_recv)
    pl.when(has_after)(hb.wait_recv)
    face_columns(hcols, hsurf, where)
    pl.when(has_after)(ha.wait_send)
    pl.when(has_before)(hb.wait_send)


def finish_kernel(hcols, w2, acc2, act, out, acc):
    acc[...] = acc2[...]
    add_faces(acc, hcols, w2)
    scale = act[0:1, :]
    for x in range(8):
        v = jnp.maximum(get(acc, slice(64 * x, 64 * x + 64)), 0.0) * scale
        out[x] = v


def body(features, occupancy, neighbours, kernel_one, kernel_two):
    total = lax.axis_size("space") * lax.axis_size("wt")
    hbm = pl.BlockSpec(memory_space=pltpu.HBM)
    vmem = pl.BlockSpec(memory_space=pltpu.VMEM)

    def pinned(v):
        return pltpu.with_memory_space_constraint(v, pltpu.HBM)

    middle = pl.pallas_call(
        functools.partial(exchange_kernel, total),
        out_shape=(
            pltpu.VMEM((6, 64, 9 * C), BF16),
            pltpu.VMEM((3, 9 * C, C), BF16),
            pltpu.VMEM((2, 512, 128), F32),
            pltpu.VMEM((8, C), F32),
        ),
        in_specs=[hbm] * 5,
        out_specs=(vmem,) * 4,
        scratch_shapes=[
            pltpu.VMEM((8, 64, C), BF16),
            pltpu.VMEM((4, 3, 64, 2 * C), BF16),
            pltpu.VMEM((4, 3, 64, 2 * C), BF16),
            pltpu.VMEM((2, 3, 3, 3, 48, 2 * C), BF16),
            pltpu.VMEM((2, 3, 3, 3, 48, 2 * C), BF16),
            pltpu.VMEM((3, 9 * C, C), BF16),
            pltpu.VMEM((10, 64, 9 * C), BF16),
            pltpu.VMEM((6, 64, 9 * C), BF16),
            pltpu.VMEM((2, 512, 128), F32),
            pltpu.SMEM((1, 27), jnp.int32),
            pltpu.SMEM((1,), jnp.int32),
            pltpu.SemaphoreType.DMA((5,)),
            pltpu.SemaphoreType.DMA((2,)),
            pltpu.SemaphoreType.DMA((2,)),
            pltpu.SemaphoreType.DMA((2,)),
            pltpu.SemaphoreType.DMA((2,)),
            pltpu.SemaphoreType.DMA((2,)),
            pltpu.SemaphoreType.DMA((2,)),
        ],
        compiler_params=pltpu.CompilerParams(
            collective_id=0, has_side_effects=True, vmem_limit_bytes=32 * 1024 * 1024),
    )(pinned(features.reshape(8, 64, C)), occupancy, pinned(neighbours), pinned(kernel_one), pinned(kernel_two))
    y = pl.pallas_call(
        finish_kernel,
        out_shape=jax.ShapeDtypeStruct((8, 64, C), F32),
        in_specs=[vmem] * 4,
        out_specs=vmem,
        scratch_shapes=[pltpu.VMEM((2, 512, 128), F32)],
        compiler_params=pltpu.CompilerParams(vmem_limit_bytes=16 * 1024 * 1024),
    )(*middle)
    return y.reshape(1, 8, 8, 8, C)


def solution(mesh):
    return jax.shard_map(
        body,
        mesh=mesh,
        in_specs=(
            P(("space", "wt"), None, None, None, None),
            P(("space", "wt")),
            P(("space", "wt"), None),
            P(None, None, None, None, "wt"),
            P(None, None, None, None, "wt"),
        ),
        out_specs=P(("space", "wt"), None, None, None, None),
        check_vma=False,
    )
```

```python
import functools

import jax
import jax.numpy as jnp
from jax import lax
from jax.experimental import pallas as pl
from jax.experimental.pallas import tpu as pltpu
from jax.sharding import PartitionSpec as P

C = 192
MESH = pl.DeviceIdType.MESH
F32 = jnp.float32
BF16 = jnp.bfloat16
FACES = ((-1, 0, 0), (1, 0, 0), (0, -1, 0), (0, 1, 0), (0, 0, -1), (0, 0, 1))


def columns(dst, low, mid, high):
    row = lax.broadcasted_iota(jnp.int32, (80, C), 0) % 8
    lo = jnp.where(row == 7, low, mid).reshape(10, 8, C)
    hi = jnp.where(row == 0, high, mid).reshape(10, 8, C)
    shifted = (pltpu.roll(lo, 1, 1).reshape(80, C), mid, pltpu.roll(hi, 7, 1).reshape(80, C))
    for inner in range(3):
        for outer in range(3):
            at = (3 * outer + inner) * C
            dst[:, at:at + C] = shifted[inner][8 * outer:8 * outer + 64].astype(BF16)


def framed(value):
    edge = jnp.zeros((8, C), F32)
    return jnp.concatenate([edge, value, edge], axis=0)


def own_columns(cols, src):
    @pl.loop(0, 8)
    def _(x):
        columns(cols.at[x + 1], 0.0, framed(src[x].astype(F32)), 0.0)


def taps(weights, chosen):
    return jnp.concatenate([weights[h, t] for t in chosen for h in range(2)], axis=0)


def own_conv(cols, weights, half):
    acc = None
    for i in range(3):
        lhs = cols[4 * half + i:4 * half + i + 4].reshape(256, 9 * C)
        d = jnp.dot(lhs, taps(weights, range(9 * i, 9 * i + 9)), preferred_element_type=F32)
        acc = d if acc is None else acc + d
    return acc


def face_columns(dst, surf, where, n):
    a, b, c = FACES[n]

    def face(p, q, r):
        pair = surf[where[9 * (p + 1) + 3 * (q + 1) + (r + 1)]]
        return (pair[:, C:] if a + b + c < 0 else pair[:, :C]).astype(F32)

    if a:
        def line(r):
            return jnp.concatenate([face(a, -1, r)[56:64], face(a, 0, r), face(a, 1, r)[0:8]], axis=0)
        columns(dst.at[n], line(-1), line(0), line(1))
    elif b:
        columns(dst.at[n], *(framed(face(0, b, r)) for r in (-1, 0, 1)))
    else:
        columns(dst.at[n], 0.0, framed(face(0, 0, c)), 0.0)


def face_product(fcols, weights, n):
    a, b, c = FACES[n]
    if a:
        chosen = [9 * (a + 1) + t for t in range(9)]
    elif b:
        chosen = [9 * i + 3 * (b + 1) + k for i in range(3) for k in range(3)]
    else:
        chosen = [9 * i + 3 * j + c + 1 for i in range(3) for j in range(3)]
    return jnp.dot(fcols[n], taps(weights, chosen), preferred_element_type=F32)


def put(acc, rows, value):
    acc[0, rows, :] = value[:, :128]
    acc[1, rows, 0:C - 128] = value[:, 128:]


def get(acc, rows):
    return jnp.concatenate([acc[0, rows, :], acc[1, rows, 0:C - 128]], axis=1)


def add_pair(acc, fcols, surf, where, weights, axis):
    for n in (2 * axis, 2 * axis + 1):
        face_columns(fcols, surf, where, n)
    for n in (2 * axis, 2 * axis + 1):
        a, b, c = FACES[n]
        d = face_product(fcols, weights, n)
        if a:
            rows = slice(0, 64) if a < 0 else slice(448, 512)
            put(acc, rows, get(acc, rows) + d)
        elif b:
            first = 0 if b < 0 else 56
            for x in range(8):
                rows = slice(64 * x + first, 64 * x + first + 8)
                put(acc, rows, get(acc, rows) + d[8 * x:8 * x + 8])
        else:
            rows = pl.ds(0 if c < 0 else 7, 64, stride=8)
            rest = jnp.concatenate([d[:, 128:], jnp.zeros((64, 256 - C), F32)], axis=1)
            for part, value in enumerate((d[:, :128], rest)):
                acc[part, rows, :] = acc[part, rows, :] + value


def pack_pair(dst, field, fix, axis):
    def rows_of(side):
        if axis == 0:
            return get(field, slice(448 * side, 448 * side + 64))
        if axis == 1:
            return jnp.concatenate(
                [get(field, slice(64 * x + 56 * side, 64 * x + 56 * side + 8)) for x in range(8)], axis=0)
        rows = pl.ds(7 * side, 64, stride=8)
        return jnp.concatenate([field[0, rows, :], field[1, rows, :][:, 0:C - 128]], axis=1)

    dst[:, :C] = fix(rows_of(0))
    dst[:, C:] = fix(rows_of(1))


def exchange_kernel(
    total, feat, occ, nbr, wk1, wk2,
    acc2, act,
    own, fx, fy, fz, hx, hy, hz, stage1, stage2, w1, w2, cols, fcols, acc, tab, occs,
    lsem, fsend, frecv, wsend, wrecv, hsend, hrecv,
):
    space = lax.axis_index("space")
    core = lax.axis_index("wt")
    mate = 1 - core
    fsurf = (fx, fy, fz)
    hsurf = (hx, hy, hz)
    me = space * 2 + core
    after = me + 1
    before = me - 1
    has_after = after < total
    has_before = before >= 0
    after_id = (after // 2, after % 2)
    before_id = (lax.max(before, 0) // 2, lax.max(before, 0) % 2)

    barrier = pltpu.get_barrier_semaphore()

    @pl.when(has_after)
    def _():
        pl.semaphore_signal(barrier, inc=1, device_id=after_id, device_id_type=MESH)

    @pl.when(has_before)
    def _():
        pl.semaphore_signal(barrier, inc=1, device_id=before_id, device_id_type=MESH)

    local = [
        pltpu.make_async_copy(feat, own, lsem.at[0]),
        pltpu.make_async_copy(nbr, tab, lsem.at[1]),
        pltpu.make_async_copy(occ, occs, lsem.at[2]),
        pltpu.make_async_copy(wk1, stage1, lsem.at[3]),
        pltpu.make_async_copy(wk2, stage2, lsem.at[4]),
    ]
    for copy in local:
        copy.start()

    for surf in fsurf + hsurf:
        surf[0] = jnp.zeros((64, 2 * C), BF16)
    cols[0] = jnp.zeros((64, 9 * C), BF16)
    cols[9] = jnp.zeros((64, 9 * C), BF16)

    local[0].wait()
    for x in range(8):
        put(acc, slice(64 * x, 64 * x + 64), own[x].astype(F32))
    for axis in range(3):
        pack_pair(fsurf[axis].at[2], acc, lambda v: v.astype(BF16), axis)

    def unpack(stage, weights):
        @pl.loop(0, 3)
        def _(i):
            for jk in range(9):
                tile = stage[i, jk // 3, jk % 3]
                weights[core, 9 * i + jk, 0:48, :] = tile[:, 0:C]
                weights[core, 9 * i + jk, 48:96, :] = tile[:, C:2 * C]

    local[3].wait()
    unpack(stage1, w1)

    pl.semaphore_wait(barrier, has_after.astype(jnp.int32) + has_before.astype(jnp.int32))

    def sends(surf, sems, recvs, axis):
        ahead = pltpu.make_async_remote_copy(
            src_ref=surf[axis].at[2], dst_ref=surf[axis].at[1],
            send_sem=sems.at[0, axis], recv_sem=recvs.at[0, axis],
            device_id=after_id, device_id_type=MESH)
        back = pltpu.make_async_remote_copy(
            src_ref=surf[axis].at[2], dst_ref=surf[axis].at[3],
            send_sem=sems.at[1, axis], recv_sem=recvs.at[1, axis],
            device_id=before_id, device_id_type=MESH)
        return ahead, back

    fcopies = [sends(fsurf, fsend, frecv, axis) for axis in range(3)]
    hcopies = [sends(hsurf, hsend, hrecv, axis) for axis in range(3)]

    def start(pair):
        pl.when(has_after)(pair[0].start)
        pl.when(has_before)(pair[1].start)

    def received(pair):
        pl.when(has_before)(pair[0].wait_recv)
        pl.when(has_after)(pair[1].wait_recv)

    def sent(pair):
        pl.when(has_after)(pair[0].wait_send)
        pl.when(has_before)(pair[1].wait_send)

    wcopies = [
        pltpu.make_async_remote_copy(
            src_ref=w.at[core], dst_ref=w.at[core], send_sem=wsend.at[n], recv_sem=wrecv.at[n],
            device_id=(space, mate), device_id_type=MESH)
        for n, w in enumerate((w1, w2))
    ]
    for pair in fcopies:
        start(pair)
    wcopies[0].start()

    local[1].wait()
    local[2].wait()
    where = []
    for t in range(27):
        n = tab[0, t]
        where.append(jnp.where(n >= 0, jnp.clip(n - me + 2, 1, 3), 0))
    active = occs[0].astype(F32)

    own_columns(cols, own)
    local[4].wait()
    unpack(stage2, w2)
    wcopies[1].start()
    wcopies[0].wait_recv()
    for half in range(2):
        put(acc, slice(256 * half, 256 * half + 256), own_conv(cols, w1, half))
    for axis in range(3):
        received(fcopies[axis])
        add_pair(acc, fcols, fsurf[axis], where, w1, axis)

    def hidden(v):
        return (jnp.maximum(v, 0.0) * active).astype(BF16)

    for axis in range(3):
        pack_pair(hsurf[axis].at[2], acc, hidden, axis)
        start(hcopies[axis])

    @pl.loop(0, 8)
    def _(x):
        v = hidden(get(acc, pl.ds(pl.multiple_of(64 * x, 64), 64)))
        columns(cols.at[x + 1], 0.0, framed(v.astype(F32)), 0.0)

    wcopies[1].wait_recv()
    for half in range(2):
        res = own[4 * half:4 * half + 4].reshape(256, C).astype(F32)
        put(acc2, slice(256 * half, 256 * half + 256), res + own_conv(cols, w2, half))
    act[...] = jnp.full((8, C), active, F32)

    for copy in wcopies:
        copy.wait_send()
    for pair in fcopies:
        sent(pair)
    for axis in range(3):
        received(hcopies[axis])
        add_pair(acc2, fcols, hsurf[axis], where, w2, axis)
    for pair in hcopies:
        sent(pair)


def finish_kernel(acc2, act, out, done, sem):
    scale = act[0:1, :]
    copies = []
    for part in range(4):
        for x in (2 * part, 2 * part + 1):
            done[x] = jnp.maximum(get(acc2, slice(64 * x, 64 * x + 64)), 0.0) * scale
        rows = pl.ds(2 * part, 2)
        copies.append(pltpu.make_async_copy(done.at[rows], out.at[rows], sem.at[part]))
        copies[part].start()
    for copy in copies:
        copy.wait()


def body(features, occupancy, neighbours, kernel_one, kernel_two):
    total = lax.axis_size("space") * lax.axis_size("wt")
    hbm = pl.BlockSpec(memory_space=pltpu.HBM)
    vmem = pl.BlockSpec(memory_space=pltpu.VMEM)

    def pinned(v):
        return pltpu.with_memory_space_constraint(v, pltpu.HBM)

    middle = pl.pallas_call(
        functools.partial(exchange_kernel, total),
        out_shape=(
            pltpu.VMEM((2, 512, 128), F32),
            pltpu.VMEM((8, C), F32),
        ),
        in_specs=[hbm] * 5,
        out_specs=(vmem,) * 2,
        scratch_shapes=[
            pltpu.VMEM((8, 64, C), BF16),
            *[pltpu.VMEM((4, 64, 2 * C), BF16)] * 6,
            pltpu.VMEM((3, 3, 3, 48, 2 * C), BF16),
            pltpu.VMEM((3, 3, 3, 48, 2 * C), BF16),
            pltpu.VMEM((2, 27, 96, C), BF16),
            pltpu.VMEM((2, 27, 96, C), BF16),
            pltpu.VMEM((10, 64, 9 * C), BF16),
            pltpu.VMEM((6, 64, 9 * C), BF16),
            pltpu.VMEM((2, 512, 128), F32),
            pltpu.SMEM((1, 27), jnp.int32),
            pltpu.SMEM((1,), jnp.int32),
            pltpu.SemaphoreType.DMA((5,)),
            pltpu.SemaphoreType.DMA((2, 3)),
            pltpu.SemaphoreType.DMA((2, 3)),
            pltpu.SemaphoreType.DMA((2,)),
            pltpu.SemaphoreType.DMA((2,)),
            pltpu.SemaphoreType.DMA((2, 3)),
            pltpu.SemaphoreType.DMA((2, 3)),
        ],
        compiler_params=pltpu.CompilerParams(
            collective_id=0, has_side_effects=True, vmem_limit_bytes=32 * 1024 * 1024),
    )(pinned(features.reshape(8, 64, C)), occupancy, pinned(neighbours), pinned(kernel_one), pinned(kernel_two))
    y = pl.pallas_call(
        finish_kernel,
        out_shape=jax.ShapeDtypeStruct((8, 64, C), F32),
        in_specs=[vmem] * 2,
        out_specs=hbm,
        scratch_shapes=[pltpu.VMEM((8, 64, C), F32), pltpu.SemaphoreType.DMA((4,))],
        compiler_params=pltpu.CompilerParams(vmem_limit_bytes=16 * 1024 * 1024),
    )(*middle)
    return y.reshape(1, 8, 8, 8, C)


def solution(mesh):
    return jax.shard_map(
        body,
        mesh=mesh,
        in_specs=(
            P(("space", "wt"), None, None, None, None),
            P(("space", "wt")),
            P(("space", "wt"), None),
            P(None, None, None, None, "wt"),
            P(None, None, None, None, "wt"),
        ),
        out_specs=P(("space", "wt"), None, None, None, None),
        check_vma=False,
    )
```

```python
import functools

import jax
import jax.numpy as jnp
from jax import lax
from jax.experimental import pallas as pl
from jax.experimental.pallas import tpu as pltpu
from jax.sharding import PartitionSpec as P

C = 192
MESH = pl.DeviceIdType.MESH
F32 = jnp.float32
BF16 = jnp.bfloat16
ROW = 32
FACES = ((-1, 0, 0), (1, 0, 0), (0, -1, 0), (0, 1, 0), (0, 0, -1), (0, 0, 1))


def columns(dst, low, mid, high):
    row = lax.broadcasted_iota(jnp.int32, (80, C), 0) % 8
    lo = jnp.where(row == 7, low, mid).reshape(10, 8, C)
    hi = jnp.where(row == 0, high, mid).reshape(10, 8, C)
    shifted = (pltpu.roll(lo, 1, 1).reshape(80, C), mid, pltpu.roll(hi, 7, 1).reshape(80, C))
    for inner in range(3):
        for outer in range(3):
            at = (3 * outer + inner) * C
            dst[:, at:at + C] = shifted[inner][8 * outer:8 * outer + 64].astype(BF16)


def framed(value):
    edge = jnp.zeros((8, C), F32)
    return jnp.concatenate([edge, value, edge], axis=0)


def own_columns(dst, value):
    columns(dst, 0.0, framed(value.astype(F32)), 0.0)


def taps(weights, chosen):
    return jnp.concatenate([weights[h, t] for t in chosen for h in range(2)], axis=0)


def own_product(cols, weights, i, first, last):
    lhs = cols[first + i - 1:last + i - 1].reshape(64 * (last - first), 9 * C)
    return jnp.dot(lhs, taps(weights, range(9 * i, 9 * i + 9)), preferred_element_type=F32)


def face_columns(dst, surf, where, n):
    a, b, c = FACES[n]

    def face(p, q, r):
        pair = surf[where[9 * (p + 1) + 3 * (q + 1) + (r + 1)]]
        return (pair[:, C:] if a + b + c < 0 else pair[:, :C]).astype(F32)

    if a:
        def line(r):
            return jnp.concatenate([face(a, -1, r)[56:64], face(a, 0, r), face(a, 1, r)[0:8]], axis=0)
        columns(dst.at[n], line(-1), line(0), line(1))
    elif b:
        columns(dst.at[n], *(framed(face(0, b, r)) for r in (-1, 0, 1)))
    else:
        columns(dst.at[n], 0.0, framed(face(0, 0, c)), 0.0)


def face_product(fcols, weights, n):
    a, b, c = FACES[n]
    if a:
        chosen = [9 * (a + 1) + t for t in range(9)]
    elif b:
        chosen = [9 * i + 3 * (b + 1) + k for i in range(3) for k in range(3)]
    else:
        chosen = [9 * i + 3 * j + c + 1 for i in range(3) for j in range(3)]
    return jnp.dot(fcols[n], taps(weights, chosen), preferred_element_type=F32)


def put(acc, rows, value):
    acc[0, rows, :] = value[:, :128]
    acc[1, rows, 0:C - 128] = value[:, 128:]


def get(acc, rows):
    return jnp.concatenate([acc[0, rows, :], acc[1, rows, 0:C - 128]], axis=1)


def add_pair(acc, fcols, weights, axis):
    for n in (2 * axis, 2 * axis + 1):
        a, b, c = FACES[n]
        d = face_product(fcols, weights, n)
        if a:
            rows = slice(0, 64) if a < 0 else slice(448, 512)
            put(acc, rows, get(acc, rows) + d)
        elif b:
            first = 0 if b < 0 else 56
            for x in range(8):
                rows = slice(64 * x + first, 64 * x + first + 8)
                put(acc, rows, get(acc, rows) + d[8 * x:8 * x + 8])
        else:
            rows = pl.ds(0 if c < 0 else 7, 64, stride=8)
            rest = jnp.concatenate([d[:, 128:], jnp.zeros((64, 256 - C), F32)], axis=1)
            for part, value in enumerate((d[:, :128], rest)):
                acc[part, rows, :] = acc[part, rows, :] + value


def add_faces(acc, fcols, surf, where, weights, arrived):
    for axis in range(3):
        arrived(axis)
        if axis:
            add_pair(acc, fcols, weights, axis - 1)
        for n in (2 * axis, 2 * axis + 1):
            face_columns(fcols, surf[axis], where, n)
    add_pair(acc, fcols, weights, 2)


def pack_pair(dst, field, fix, axis):
    def rows_of(side):
        if axis == 0:
            return get(field, slice(448 * side, 448 * side + 64))
        if axis == 1:
            return jnp.concatenate(
                [get(field, slice(64 * x + 56 * side, 64 * x + 56 * side + 8)) for x in range(8)], axis=0)
        rows = pl.ds(7 * side, 64, stride=8)
        return jnp.concatenate([field[0, rows, :], field[1, rows, :][:, 0:C - 128]], axis=1)

    dst[:, :C] = fix(rows_of(0))
    dst[:, C:] = fix(rows_of(1))


def exchange_kernel(
    total, feat, occ, nbr, wk1, wk2,
    acc2, act,
    own, fx, fy, fz, ex, ey, ez, hx, hy, hz, stage1, stage2, w1, w2, cols, fcols, acc, facc,
    px, py, pz, qx, qy, qz, ftab, tab, tab2, occs,
    lsem, fsend, frecv, wsend, wrecv, hsend, hrecv, psend, precv,
):
    space = lax.axis_index("space")
    core = lax.axis_index("wt")
    chips = total // 2
    me = space * 2 + core
    mate = 1 - core
    mate_slot = space * 2 + mate
    step = 2 * core - 1
    far = space + step
    has_far = (far >= 0) & (far < chips)
    far_id = (jnp.clip(far, 0, chips - 1), mate)
    mate_id = (space, mate)
    long = has_far & ((space + core) % ROW == 0)
    short = has_far & jnp.logical_not(long)
    fsurf = (fx, fy, fz)
    esurf = (ex, ey, ez)
    hsurf = (hx, hy, hz)
    sums = (px, py, pz)
    far_sums = (qx, qy, qz)

    barrier = pltpu.get_barrier_semaphore()
    pl.semaphore_signal(barrier, inc=1, device_id=mate_id, device_id_type=MESH)

    @pl.when(has_far)
    def _():
        pl.semaphore_signal(barrier, inc=1, device_id=far_id, device_id_type=MESH)

    local = [
        pltpu.make_async_copy(feat, own, lsem.at[0]),
        pltpu.make_async_copy(nbr, tab, lsem.at[1]),
        pltpu.make_async_copy(occ, occs, lsem.at[2]),
        pltpu.make_async_copy(wk1, stage1, lsem.at[3]),
        pltpu.make_async_copy(wk2, stage2, lsem.at[4]),
    ]
    for copy in local:
        copy.start()

    for surf in fsurf + esurf + hsurf:
        surf[0] = jnp.zeros((64, 2 * C), BF16)

    local[0].wait()
    for x in range(8):
        put(acc, slice(64 * x, 64 * x + 64), own[x].astype(F32))
    for axis in range(3):
        pack_pair(fsurf[axis].at[2], acc, lambda v: v.astype(BF16), axis)

    def unpack(stage, weights, i):
        for jk in range(9):
            tile = stage[i, jk // 3, jk % 3]
            weights[core, 9 * i + jk, 0:48, :] = tile[:, 0:C]
            weights[core, 9 * i + jk, 48:96, :] = tile[:, C:2 * C]

    pl.semaphore_wait(barrier, 1 + has_far.astype(jnp.int32))

    def remote(source, target, send, recv, device):
        return pltpu.make_async_remote_copy(
            src_ref=source, dst_ref=target, send_sem=send, recv_sem=recv,
            device_id=device, device_id_type=MESH)

    def sends(surf, sems, recvs, axis):
        return (
            remote(surf[axis].at[2], surf[axis].at[1], sems.at[0, axis], recvs.at[0, axis], mate_id),
            remote(surf[axis].at[2], surf[axis].at[3], sems.at[1, axis], recvs.at[1, axis], far_id),
        )

    fcopies = [sends(fsurf, fsend, frecv, axis) for axis in range(3)]
    hcopies = [sends(hsurf, hsend, hrecv, axis) for axis in range(3)]
    ecopies = [
        remote(fsurf[axis].at[2], esurf[axis].at[1], fsend.at[1, axis], frecv.at[1, axis], far_id)
        for axis in range(3)]
    pcopies = [
        remote(sums[axis], far_sums[axis], psend.at[axis], precv.at[axis], far_id) for axis in range(3)]
    tcopy = remote(nbr, ftab, psend.at[3], precv.at[3], far_id)

    def to_mate(part, n):
        return remote(part, part, wsend.at[n], wrecv.at[n], mate_id)

    order = (1, 0, 2)
    wcopies = [to_mate(w1.at[core, pl.ds(9 * i, 9)], n) for n, i in enumerate(order)]
    wcopies.append(to_mate(w2.at[core], 3))
    for axis in range(3):
        pl.when(short)(fcopies[axis][1].start)
        pl.when(long)(ecopies[axis].start)
        fcopies[axis][0].start()
    pl.when(long)(tcopy.start)
    local[3].wait()
    for n, i in enumerate(order):
        unpack(stage1, w1, i)
        wcopies[n].start()

    local[1].wait()
    local[2].wait()
    where = []
    for t in range(27):
        n = tab[0, t]
        where.append(jnp.where(n < 0, 0, jnp.where(n == me, 2, jnp.where(n == mate_slot, 1, 3))))
    active = occs[0].astype(F32)

    for x in range(8):
        own_columns(cols.at[x], own[x])
    local[4].wait()
    for n, i in enumerate(order):
        wcopies[n].wait_recv()
        unpack(stage2, w2, i)
        for first, last in (((1, 4), (4, 8)), ((0, 4), (4, 8)), ((0, 4), (4, 7)))[i]:
            rows = slice(64 * first, 64 * last)
            d = own_product(cols, w1, i, first, last)
            put(acc, rows, get(acc, rows) + d if n else d)
    wcopies[3].start()

    @pl.when(jnp.logical_not(long))
    def _():
        def arrived(axis):
            fcopies[axis][0].wait_recv()
            pl.when(short)(fcopies[axis][1].wait_recv)

        add_faces(acc, fcols, fsurf, where, w1, arrived)

    @pl.when(long)
    def _():
        near = [jnp.where(w == 3, 0, w) for w in where]
        add_faces(acc, fcols, fsurf, near, w1, lambda axis: fcopies[axis][0].wait_recv())
        for axis in range(3):
            pack_pair(sums[axis], acc, lambda v: v, axis)
            pcopies[axis].start()
        away = [jnp.where(w == 3, 1, 0) for w in where]
        add_faces(acc, fcols, esurf, away, w1, lambda axis: ecopies[axis].wait_recv())

    def hidden(v):
        return (jnp.maximum(v, 0.0) * active).astype(BF16)

    for axis in range(3):
        pack_pair(hsurf[axis].at[2], acc, hidden, axis)
        pl.when(short)(hcopies[axis][1].start)
        hcopies[axis][0].start()

    wcopies[3].wait_recv()
    for x in range(8):
        own_columns(cols.at[x], hidden(get(acc, slice(64 * x, 64 * x + 64))))
    res = own[0:4].reshape(256, C).astype(F32)
    d = own_product(cols, w2, 1, 0, 4) + own_product(cols, w2, 2, 0, 4) + res
    put(acc2, slice(0, 64), d[:64])
    put(acc2, slice(64, 256), d[64:] + own_product(cols, w2, 0, 1, 4))
    res = own[4:8].reshape(256, C).astype(F32)
    d = own_product(cols, w2, 1, 4, 8) + own_product(cols, w2, 0, 4, 8) + res
    put(acc2, slice(256, 448), d[:192] + own_product(cols, w2, 2, 4, 7))
    put(acc2, slice(448, 512), d[192:])
    act[...] = jnp.full((8, C), active, F32)

    @pl.when(long)
    def _():
        tcopy.wait_recv()
        fetch = pltpu.make_async_copy(ftab, tab2, lsem.at[5])
        fetch.start()
        facc[...] = jnp.zeros((2, 512, 128), F32)
        fetch.wait()
        given = [jnp.where(tab2[0, t] == me, 2, 0) for t in range(27)]
        add_faces(facc, fcols, fsurf, given, w1, lambda axis: None)
        for axis in range(3):
            pcopies[axis].wait_send()
        for axis in range(3):
            pack_pair(sums[axis], facc, lambda v: v, axis)

    for copy in wcopies:
        copy.wait_send()
    for axis in range(3):
        fcopies[axis][0].wait_send()
        pl.when(short)(fcopies[axis][1].wait_send)
        pl.when(long)(ecopies[axis].wait_send)
    pl.when(long)(tcopy.wait_send)

    def arrived(axis):
        hcopies[axis][0].wait_recv()
        pl.when(short)(hcopies[axis][1].wait_recv)

        @pl.when(long)
        def _():
            pcopies[axis].wait_recv()
            hsurf[axis][3] = jnp.maximum(far_sums[axis][...] + sums[axis][...], 0.0).astype(BF16)

    add_faces(acc2, fcols, hsurf, where, w2, arrived)
    for near, away in hcopies:
        near.wait_send()
        pl.when(short)(away.wait_send)


def finish_kernel(acc2, act, out, done, sem):
    scale = act[0:1, :]
    copies = []
    for part in range(4):
        for x in (2 * part, 2 * part + 1):
            done[x] = jnp.maximum(get(acc2, slice(64 * x, 64 * x + 64)), 0.0) * scale
        rows = pl.ds(2 * part, 2)
        copies.append(pltpu.make_async_copy(done.at[rows], out.at[rows], sem.at[part]))
        copies[part].start()
    for copy in copies:
        copy.wait()


def body(features, occupancy, neighbours, kernel_one, kernel_two):
    total = lax.axis_size("space") * lax.axis_size("wt")
    hbm = pl.BlockSpec(memory_space=pltpu.HBM)
    vmem = pl.BlockSpec(memory_space=pltpu.VMEM)

    def pinned(v):
        return pltpu.with_memory_space_constraint(v, pltpu.HBM)

    middle = pl.pallas_call(
        functools.partial(exchange_kernel, total),
        out_shape=(
            pltpu.VMEM((2, 512, 128), F32),
            pltpu.VMEM((8, C), F32),
        ),
        in_specs=[hbm] * 5,
        out_specs=(vmem,) * 2,
        scratch_shapes=[
            pltpu.VMEM((8, 64, C), BF16),
            *[pltpu.VMEM((4, 64, 2 * C), BF16)] * 3,
            *[pltpu.VMEM((2, 64, 2 * C), BF16)] * 3,
            *[pltpu.VMEM((4, 64, 2 * C), BF16)] * 3,
            pltpu.VMEM((3, 3, 3, 48, 2 * C), BF16),
            pltpu.VMEM((3, 3, 3, 48, 2 * C), BF16),
            pltpu.VMEM((2, 27, 96, C), BF16),
            pltpu.VMEM((2, 27, 96, C), BF16),
            pltpu.VMEM((8, 64, 9 * C), BF16),
            pltpu.VMEM((6, 64, 9 * C), BF16),
            pltpu.VMEM((2, 512, 128), F32),
            pltpu.VMEM((2, 512, 128), F32),
            *[pltpu.VMEM((64, 2 * C), F32)] * 6,
            pltpu.VMEM((1, 27), jnp.int32),
            pltpu.SMEM((1, 27), jnp.int32),
            pltpu.SMEM((1, 27), jnp.int32),
            pltpu.SMEM((1,), jnp.int32),
            pltpu.SemaphoreType.DMA((6,)),
            pltpu.SemaphoreType.DMA((2, 3)),
            pltpu.SemaphoreType.DMA((2, 3)),
            pltpu.SemaphoreType.DMA((4,)),
            pltpu.SemaphoreType.DMA((4,)),
            pltpu.SemaphoreType.DMA((2, 3)),
            pltpu.SemaphoreType.DMA((2, 3)),
            pltpu.SemaphoreType.DMA((4,)),
            pltpu.SemaphoreType.DMA((4,)),
        ],
        compiler_params=pltpu.CompilerParams(
            collective_id=0, has_side_effects=True, vmem_limit_bytes=32 * 1024 * 1024),
    )(pinned(features.reshape(8, 64, C)), occupancy, pinned(neighbours), pinned(kernel_one), pinned(kernel_two))
    y = pl.pallas_call(
        finish_kernel,
        out_shape=jax.ShapeDtypeStruct((8, 64, C), F32),
        in_specs=[vmem] * 2,
        out_specs=hbm,
        scratch_shapes=[pltpu.VMEM((8, 64, C), F32), pltpu.SemaphoreType.DMA((4,))],
        compiler_params=pltpu.CompilerParams(vmem_limit_bytes=16 * 1024 * 1024),
    )(*middle)
    return y.reshape(1, 8, 8, 8, C)


def solution(mesh):
    return jax.shard_map(
        body,
        mesh=mesh,
        in_specs=(
            P(("space", "wt"), None, None, None, None),
            P(("space", "wt")),
            P(("space", "wt"), None),
            P(None, None, None, None, "wt"),
            P(None, None, None, None, "wt"),
        ),
        out_specs=P(("space", "wt"), None, None, None, None),
        check_vma=False,
    )
```

```python
import functools

import jax
import jax.numpy as jnp
from jax import lax
from jax.experimental import pallas as pl
from jax.experimental.pallas import tpu as pltpu
from jax.sharding import PartitionSpec as P

C = 192
MESH = pl.DeviceIdType.MESH
F32 = jnp.float32
BF16 = jnp.bfloat16
ROW = 32
FACES = ((-1, 0, 0), (1, 0, 0), (0, -1, 0), (0, 1, 0), (0, 0, -1), (0, 0, 1))


def columns(dst, low, mid, high):
    row = lax.broadcasted_iota(jnp.int32, (80, C), 0) % 8
    lo = jnp.where(row == 7, low, mid).reshape(10, 8, C)
    hi = jnp.where(row == 0, high, mid).reshape(10, 8, C)
    shifted = (pltpu.roll(lo, 1, 1).reshape(80, C), mid, pltpu.roll(hi, 7, 1).reshape(80, C))
    for inner in range(3):
        for outer in range(3):
            at = (3 * outer + inner) * C
            dst[:, at:at + C] = shifted[inner][8 * outer:8 * outer + 64].astype(BF16)


def framed(value):
    edge = jnp.zeros((8, C), F32)
    return jnp.concatenate([edge, value, edge], axis=0)


def own_columns(dst, value):
    columns(dst, 0.0, framed(value.astype(F32)), 0.0)


def taps(weights, chosen):
    return jnp.concatenate([weights[h, t] for t in chosen for h in range(2)], axis=0)


def own_product(cols, weights, i, first, last):
    lhs = cols[first + i - 1:last + i - 1].reshape(64 * (last - first), 9 * C)
    return jnp.dot(lhs, taps(weights, range(9 * i, 9 * i + 9)), preferred_element_type=F32)


def face_columns(dst, surf, where, n):
    a, b, c = FACES[n]

    def face(p, q, r):
        pair = surf[where[9 * (p + 1) + 3 * (q + 1) + (r + 1)]]
        return (pair[:, C:] if a + b + c < 0 else pair[:, :C]).astype(F32)

    if a:
        def line(r):
            return jnp.concatenate([face(a, -1, r)[56:64], face(a, 0, r), face(a, 1, r)[0:8]], axis=0)
        columns(dst.at[n], line(-1), line(0), line(1))
    elif b:
        columns(dst.at[n], *(framed(face(0, b, r)) for r in (-1, 0, 1)))
    else:
        columns(dst.at[n], 0.0, framed(face(0, 0, c)), 0.0)


def face_product(fcols, weights, n):
    a, b, c = FACES[n]
    if a:
        chosen = [9 * (a + 1) + t for t in range(9)]
    elif b:
        chosen = [9 * i + 3 * (b + 1) + k for i in range(3) for k in range(3)]
    else:
        chosen = [9 * i + 3 * j + c + 1 for i in range(3) for j in range(3)]
    return jnp.dot(fcols[n], taps(weights, chosen), preferred_element_type=F32)


def put(acc, rows, value):
    acc[0, rows, :] = value[:, :128]
    acc[1, rows, 0:C - 128] = value[:, 128:]


def get(acc, rows):
    return jnp.concatenate([acc[0, rows, :], acc[1, rows, 0:C - 128]], axis=1)


def add_pair(acc, fcols, weights, axis):
    for n in (2 * axis, 2 * axis + 1):
        a, b, c = FACES[n]
        d = face_product(fcols, weights, n)
        if a:
            rows = slice(0, 64) if a < 0 else slice(448, 512)
            put(acc, rows, get(acc, rows) + d)
        elif b:
            first = 0 if b < 0 else 56
            for x in range(8):
                rows = slice(64 * x + first, 64 * x + first + 8)
                put(acc, rows, get(acc, rows) + d[8 * x:8 * x + 8])
        else:
            rows = pl.ds(0 if c < 0 else 7, 64, stride=8)
            rest = jnp.concatenate([d[:, 128:], jnp.zeros((64, 256 - C), F32)], axis=1)
            for part, value in enumerate((d[:, :128], rest)):
                acc[part, rows, :] = acc[part, rows, :] + value


def add_faces(acc, fcols, surf, where, weights, arrived):
    for axis in range(3):
        arrived(axis)
        if axis:
            add_pair(acc, fcols, weights, axis - 1)
        for n in (2 * axis, 2 * axis + 1):
            face_columns(fcols, surf[axis], where, n)
    add_pair(acc, fcols, weights, 2)


def pack_pair(dst, field, fix, axis):
    def rows_of(side):
        if axis == 0:
            return get(field, slice(448 * side, 448 * side + 64))
        if axis == 1:
            return jnp.concatenate(
                [get(field, slice(64 * x + 56 * side, 64 * x + 56 * side + 8)) for x in range(8)], axis=0)
        rows = pl.ds(7 * side, 64, stride=8)
        return jnp.concatenate([field[0, rows, :], field[1, rows, :][:, 0:C - 128]], axis=1)

    dst[:, :C] = fix(rows_of(0))
    dst[:, C:] = fix(rows_of(1))


def exchange_kernel(
    total, feat, occ, nbr, wk1, wk2,
    acc2, act,
    own, fx, fy, fz, ex, ey, ez, hx, hy, hz, stage1, mate1, stage2, w1, w2, cols, fcols, acc, facc,
    px, py, pz, qx, qy, qz, gx, gy, gz, ftab, tab, tab2, occs,
    lsem, fsend, frecv, wsend, wrecv, hsend, hrecv, psend, precv,
):
    space = lax.axis_index("space")
    core = lax.axis_index("wt")
    chips = total // 2
    me = space * 2 + core
    mate = 1 - core
    mate_slot = space * 2 + mate
    step = 2 * core - 1
    far = space + step
    has_far = (far >= 0) & (far < chips)
    far_id = (jnp.clip(far, 0, chips - 1), mate)
    mate_id = (space, mate)
    long = has_far & ((space + core) % ROW == 0)
    short = has_far & jnp.logical_not(long)
    early = long | (has_far & ((space + core) % 4 == 0)) | (me == 1)
    first = long & (core == 0)
    second = long & (core == 1)
    fsurf = (fx, fy, fz)
    esurf = (ex, ey, ez)
    hsurf = (hx, hy, hz)
    sums = (px, py, pz)
    far_sums = (qx, qy, qz)
    given_sums = (gx, gy, gz)

    barrier = pltpu.get_barrier_semaphore()
    pl.semaphore_signal(barrier, inc=1, device_id=mate_id, device_id_type=MESH)

    @pl.when(has_far)
    def _():
        pl.semaphore_signal(barrier, inc=1, device_id=far_id, device_id_type=MESH)

    local = [
        pltpu.make_async_copy(feat, own, lsem.at[0]),
        pltpu.make_async_copy(nbr, tab, lsem.at[1]),
        pltpu.make_async_copy(occ, occs, lsem.at[2]),
        pltpu.make_async_copy(wk1, stage1, lsem.at[3]),
        pltpu.make_async_copy(wk2, stage2, lsem.at[4]),
    ]
    for copy in local:
        copy.start()

    for surf in fsurf + esurf + hsurf:
        surf[0] = jnp.zeros((64, 2 * C), BF16)

    def unpack(stage, weights, h, i):
        for jk in range(9):
            tile = stage[i, jk // 3, jk % 3]
            weights[h, 9 * i + jk, 0:48, :] = tile[:, 0:C]
            weights[h, 9 * i + jk, 48:96, :] = tile[:, C:2 * C]

    def remote(source, target, send, recv, device):
        return pltpu.make_async_remote_copy(
            src_ref=source, dst_ref=target, send_sem=send, recv_sem=recv,
            device_id=device, device_id_type=MESH)

    def sends(surf, sems, recvs, axis):
        return (
            remote(surf[axis].at[2], surf[axis].at[1], sems.at[0, axis], recvs.at[0, axis], mate_id),
            remote(surf[axis].at[2], surf[axis].at[3], sems.at[1, axis], recvs.at[1, axis], far_id),
        )

    fcopies = [sends(fsurf, fsend, frecv, axis) for axis in range(3)]
    hcopies = [sends(hsurf, hsend, hrecv, axis) for axis in range(3)]
    ecopies = [
        remote(fsurf[axis].at[2], esurf[axis].at[1], fsend.at[1, axis], frecv.at[1, axis], far_id)
        for axis in range(3)]
    pcopies = [
        remote(sums[axis], far_sums[axis], psend.at[axis], precv.at[axis], far_id) for axis in range(3)]
    tcopy = remote(nbr, ftab, psend.at[3], precv.at[3], far_id)

    order = (1, 0, 2)
    wcopies = [
        remote(wk1.at[i], mate1.at[i], wsend.at[n], wrecv.at[n], mate_id) for n, i in enumerate(order)]
    for n, i in enumerate(order):
        part = w2.at[core, pl.ds(9 * i, 9)]
        wcopies.append(remote(part, part, wsend.at[3 + n], wrecv.at[3 + n], mate_id))

    def prepare_faces():
        local[0].wait()
        for x in range(8):
            put(acc, slice(64 * x, 64 * x + 64), own[x].astype(F32))
        for axis in range(3):
            pack_pair(fsurf[axis].at[2], acc, lambda v: v.astype(BF16), axis)

    def prepare_own():
        for x in range(8):
            own_columns(cols.at[x], own[x])
        local[3].wait()
        for i in order:
            unpack(stage1, w1, core, i)

    def unpack_two():
        local[4].wait()
        for i in order:
            unpack(stage2, w2, core, i)

    def send_two():
        for n in range(3):
            wcopies[3 + n].start()

    def own_part(with_two=True, send=True):
        if with_two:
            local[4].wait()
        for n, i in enumerate(order):
            wcopies[n].wait_recv()
            unpack(mate1, w1, mate, i)
            if with_two:
                unpack(stage2, w2, core, i)
            for start, stop in (((1, 4), (4, 8)), ((0, 4), (4, 8)), ((0, 4), (4, 7)))[i]:
                rows = slice(64 * start, 64 * stop)
                d = own_product(cols, w1, i, start, stop)
                put(acc, rows, get(acc, rows) + d if n else d)
            if send:
                wcopies[3 + n].start()

    @pl.when(early)
    def _():
        prepare_faces()
        prepare_own()

    pl.when(first)(functools.partial(own_part, True, False))
    pl.semaphore_wait(barrier, 1 + has_far.astype(jnp.int32))

    @pl.when(jnp.logical_not(early))
    def _():
        for n in range(3):
            wcopies[n].start()
        prepare_faces()

    pl.when(long)(tcopy.start)
    for axis in range(3):
        pl.when(short)(fcopies[axis][1].start)
        pl.when(long)(ecopies[axis].start)
        fcopies[axis][0].start()

    @pl.when(early)
    def _():
        for n in range(3):
            wcopies[n].start()

    pl.when(jnp.logical_not(early))(prepare_own)

    local[1].wait()
    local[2].wait()
    where = []
    for t in range(27):
        n = tab[0, t]
        where.append(jnp.where(n < 0, 0, jnp.where(n == me, 2, jnp.where(n == mate_slot, 1, 3))))
    active = occs[0].astype(F32)

    pl.when(jnp.logical_not(long))(own_part)
    pl.when(second)(functools.partial(own_part, False, False))
    pl.when(first)(send_two)

    @pl.when(jnp.logical_not(long))
    def _():
        def arrived(axis):
            fcopies[axis][0].wait_recv()
            pl.when(short)(fcopies[axis][1].wait_recv)

        add_faces(acc, fcols, fsurf, where, w1, arrived)

    @pl.when(long)
    def _():
        near = [jnp.where(w == 3, 0, w) for w in where]
        add_faces(acc, fcols, fsurf, near, w1, lambda axis: fcopies[axis][0].wait_recv())
        for axis in range(3):
            pack_pair(sums[axis], acc, lambda v: v.astype(BF16), axis)
            pcopies[axis].start()

        @pl.when(second)
        def _():
            unpack_two()
            send_two()

        tcopy.wait_recv()
        fetch = pltpu.make_async_copy(ftab, tab2, lsem.at[5])
        fetch.start()
        facc[...] = jnp.zeros((2, 512, 128), F32)
        fetch.wait()
        given = [jnp.where(tab2[0, t] == me, 2, 0) for t in range(27)]
        add_faces(facc, fcols, fsurf, given, w1, lambda axis: None)
        for axis in range(3):
            pack_pair(given_sums[axis], facc, lambda v: v, axis)
        away = [jnp.where(w == 3, 1, 0) for w in where]
        add_faces(acc, fcols, esurf, away, w1, lambda axis: ecopies[axis].wait_recv())

    def hidden(v):
        return (jnp.maximum(v, 0.0) * active).astype(BF16)

    for axis in range(3):
        pack_pair(hsurf[axis].at[2], acc, hidden, axis)
        pl.when(short)(hcopies[axis][1].start)
        hcopies[axis][0].start()

    for n in range(3):
        wcopies[3 + n].wait_recv()
    for x in range(8):
        own_columns(cols.at[x], hidden(get(acc, slice(64 * x, 64 * x + 64))))
    res = own[0:4].reshape(256, C).astype(F32)
    d = own_product(cols, w2, 1, 0, 4) + own_product(cols, w2, 2, 0, 4) + res
    put(acc2, slice(0, 64), d[:64])
    put(acc2, slice(64, 256), d[64:] + own_product(cols, w2, 0, 1, 4))
    res = own[4:8].reshape(256, C).astype(F32)
    d = own_product(cols, w2, 1, 4, 8) + own_product(cols, w2, 0, 4, 8) + res
    put(acc2, slice(256, 448), d[:192] + own_product(cols, w2, 2, 4, 7))
    put(acc2, slice(448, 512), d[192:])
    act[...] = jnp.full((8, C), active, F32)

    for copy in wcopies:
        copy.wait_send()
    for axis in range(3):
        fcopies[axis][0].wait_send()
        pl.when(short)(fcopies[axis][1].wait_send)
        pl.when(long)(ecopies[axis].wait_send)

    @pl.when(long)
    def _():
        tcopy.wait_send()
        for axis in range(3):
            pcopies[axis].wait_send()

    def arrived(axis):
        hcopies[axis][0].wait_recv()
        pl.when(short)(hcopies[axis][1].wait_recv)

        @pl.when(long)
        def _():
            pcopies[axis].wait_recv()
            hsurf[axis][3] = jnp.maximum(
                far_sums[axis][...].astype(F32) + given_sums[axis][...], 0.0).astype(BF16)

    add_faces(acc2, fcols, hsurf, where, w2, arrived)
    for near, away in hcopies:
        near.wait_send()
        pl.when(short)(away.wait_send)


def finish_kernel(acc2, act, out, done, sem):
    scale = act[0:1, :]
    copies = []
    for part in range(4):
        for x in (2 * part, 2 * part + 1):
            done[x] = jnp.maximum(get(acc2, slice(64 * x, 64 * x + 64)), 0.0) * scale
        rows = pl.ds(2 * part, 2)
        copies.append(pltpu.make_async_copy(done.at[rows], out.at[rows], sem.at[part]))
        copies[part].start()
    for copy in copies:
        copy.wait()


def body(features, occupancy, neighbours, kernel_one, kernel_two):
    total = lax.axis_size("space") * lax.axis_size("wt")
    hbm = pl.BlockSpec(memory_space=pltpu.HBM)
    vmem = pl.BlockSpec(memory_space=pltpu.VMEM)

    def pinned(v):
        return pltpu.with_memory_space_constraint(v, pltpu.HBM)

    middle = pl.pallas_call(
        functools.partial(exchange_kernel, total),
        out_shape=(
            pltpu.VMEM((2, 512, 128), F32),
            pltpu.VMEM((8, C), F32),
        ),
        in_specs=[hbm] * 5,
        out_specs=(vmem,) * 2,
        scratch_shapes=[
            pltpu.VMEM((8, 64, C), BF16),
            *[pltpu.VMEM((4, 64, 2 * C), BF16)] * 3,
            *[pltpu.VMEM((2, 64, 2 * C), BF16)] * 3,
            *[pltpu.VMEM((4, 64, 2 * C), BF16)] * 3,
            *[pltpu.VMEM((3, 3, 3, 48, 2 * C), BF16)] * 3,
            pltpu.VMEM((2, 27, 96, C), BF16),
            pltpu.VMEM((2, 27, 96, C), BF16),
            pltpu.VMEM((8, 64, 9 * C), BF16),
            pltpu.VMEM((6, 64, 9 * C), BF16),
            pltpu.VMEM((2, 512, 128), F32),
            pltpu.VMEM((2, 512, 128), F32),
            *[pltpu.VMEM((64, 2 * C), BF16)] * 6,
            *[pltpu.VMEM((64, 2 * C), F32)] * 3,
            pltpu.VMEM((1, 27), jnp.int32),
            pltpu.SMEM((1, 27), jnp.int32),
            pltpu.SMEM((1, 27), jnp.int32),
            pltpu.SMEM((1,), jnp.int32),
            pltpu.SemaphoreType.DMA((6,)),
            pltpu.SemaphoreType.DMA((2, 3)),
            pltpu.SemaphoreType.DMA((2, 3)),
            pltpu.SemaphoreType.DMA((6,)),
            pltpu.SemaphoreType.DMA((6,)),
            pltpu.SemaphoreType.DMA((2, 3)),
            pltpu.SemaphoreType.DMA((2, 3)),
            pltpu.SemaphoreType.DMA((4,)),
            pltpu.SemaphoreType.DMA((4,)),
        ],
        compiler_params=pltpu.CompilerParams(
            collective_id=0, has_side_effects=True, vmem_limit_bytes=32 * 1024 * 1024),
    )(pinned(features.reshape(8, 64, C)), occupancy, pinned(neighbours), pinned(kernel_one), pinned(kernel_two))
    y = pl.pallas_call(
        finish_kernel,
        out_shape=jax.ShapeDtypeStruct((8, 64, C), F32),
        in_specs=[vmem] * 2,
        out_specs=hbm,
        scratch_shapes=[pltpu.VMEM((8, 64, C), F32), pltpu.SemaphoreType.DMA((4,))],
        compiler_params=pltpu.CompilerParams(vmem_limit_bytes=16 * 1024 * 1024),
    )(*middle)
    return y.reshape(1, 8, 8, 8, C)


def solution(mesh):
    return jax.shard_map(
        body,
        mesh=mesh,
        in_specs=(
            P(("space", "wt"), None, None, None, None),
            P(("space", "wt")),
            P(("space", "wt"), None),
            P(None, None, None, None, "wt"),
            P(None, None, None, None, "wt"),
        ),
        out_specs=P(("space", "wt"), None, None, None, None),
        check_vma=False,
    )
```

```python
import functools

import jax
import jax.numpy as jnp
from jax import lax
from jax.experimental import pallas as pl
from jax.experimental.pallas import tpu as pltpu
from jax.sharding import PartitionSpec as P

C = 192
MESH = pl.DeviceIdType.MESH
F32 = jnp.float32
BF16 = jnp.bfloat16
ROW = 16
FACES = ((-1, 0, 0), (1, 0, 0), (0, -1, 0), (0, 1, 0), (0, 0, -1), (0, 0, 1))


def columns(dst, low, mid, high):
    row = lax.broadcasted_iota(jnp.int32, (80, C), 0) % 8
    lo = jnp.where(row == 7, low, mid).reshape(10, 8, C)
    hi = jnp.where(row == 0, high, mid).reshape(10, 8, C)
    shifted = (pltpu.roll(lo, 1, 1).reshape(80, C), mid, pltpu.roll(hi, 7, 1).reshape(80, C))
    for inner in range(3):
        for outer in range(3):
            at = (3 * outer + inner) * C
            dst[:, at:at + C] = shifted[inner][8 * outer:8 * outer + 64].astype(BF16)


def framed(value):
    edge = jnp.zeros((8, C), F32)
    return jnp.concatenate([edge, value, edge], axis=0)


def own_columns(dst, value):
    columns(dst, 0.0, framed(value.astype(F32)), 0.0)


def taps(weights, chosen):
    return jnp.concatenate([weights[h, t] for t in chosen for h in range(2)], axis=0)


def own_product(cols, weights, i, first, last):
    lhs = cols[first + i - 1:last + i - 1].reshape(64 * (last - first), 9 * C)
    return jnp.dot(lhs, taps(weights, range(9 * i, 9 * i + 9)), preferred_element_type=F32)


def face_columns(dst, surf, where, n):
    a, b, c = FACES[n]

    def face(p, q, r):
        pair = surf[where[9 * (p + 1) + 3 * (q + 1) + (r + 1)]]
        return (pair[:, C:] if a + b + c < 0 else pair[:, :C]).astype(F32)

    if a:
        def line(r):
            return jnp.concatenate([face(a, -1, r)[56:64], face(a, 0, r), face(a, 1, r)[0:8]], axis=0)
        columns(dst.at[n], line(-1), line(0), line(1))
    elif b:
        columns(dst.at[n], *(framed(face(0, b, r)) for r in (-1, 0, 1)))
    else:
        columns(dst.at[n], 0.0, framed(face(0, 0, c)), 0.0)


def face_product(fcols, weights, n):
    a, b, c = FACES[n]
    if a:
        chosen = [9 * (a + 1) + t for t in range(9)]
    elif b:
        chosen = [9 * i + 3 * (b + 1) + k for i in range(3) for k in range(3)]
    else:
        chosen = [9 * i + 3 * j + c + 1 for i in range(3) for j in range(3)]
    return jnp.dot(fcols[n], taps(weights, chosen), preferred_element_type=F32)


def put(acc, rows, value):
    acc[0, rows, :] = value[:, :128]
    acc[1, rows, 0:C - 128] = value[:, 128:]


def get(acc, rows):
    return jnp.concatenate([acc[0, rows, :], acc[1, rows, 0:C - 128]], axis=1)


def add_pair(acc, fcols, weights, axis):
    for n in (2 * axis, 2 * axis + 1):
        a, b, c = FACES[n]
        d = face_product(fcols, weights, n)
        if a:
            rows = slice(0, 64) if a < 0 else slice(448, 512)
            put(acc, rows, get(acc, rows) + d)
        elif b:
            first = 0 if b < 0 else 56
            for x in range(8):
                rows = slice(64 * x + first, 64 * x + first + 8)
                put(acc, rows, get(acc, rows) + d[8 * x:8 * x + 8])
        else:
            rows = pl.ds(0 if c < 0 else 7, 64, stride=8)
            rest = jnp.concatenate([d[:, 128:], jnp.zeros((64, 256 - C), F32)], axis=1)
            for part, value in enumerate((d[:, :128], rest)):
                acc[part, rows, :] = acc[part, rows, :] + value


def add_faces(acc, fcols, surf, where, weights, arrived):
    for axis in range(3):
        arrived(axis)
        if axis:
            add_pair(acc, fcols, weights, axis - 1)
        for n in (2 * axis, 2 * axis + 1):
            face_columns(fcols, surf[axis], where, n)
    add_pair(acc, fcols, weights, 2)


def pack_pair(dst, field, fix, axis):
    def rows_of(side):
        if axis == 0:
            return get(field, slice(448 * side, 448 * side + 64))
        if axis == 1:
            return jnp.concatenate(
                [get(field, slice(64 * x + 56 * side, 64 * x + 56 * side + 8)) for x in range(8)], axis=0)
        rows = pl.ds(7 * side, 64, stride=8)
        return jnp.concatenate([field[0, rows, :], field[1, rows, :][:, 0:C - 128]], axis=1)

    dst[:, :C] = fix(rows_of(0))
    dst[:, C:] = fix(rows_of(1))


def exchange_kernel(
    total, feat, occ, nbr, wk1, wk2,
    acc2, act,
    own, fx, fy, fz, ex, ey, ez, hx, hy, hz, stage1, mate1, stage2, w1, w2, cols, fcols, acc, facc,
    px, py, pz, qx, qy, qz, gx, gy, gz, ftab, tab, tab2, occs,
    lsem, fsend, frecv, wsend, wrecv, hsend, hrecv, psend, precv,
):
    space = lax.axis_index("space")
    core = lax.axis_index("wt")
    chips = total // 2
    me = space * 2 + core
    mate = 1 - core
    mate_slot = space * 2 + mate
    step = 2 * core - 1
    far = space + step
    has_far = (far >= 0) & (far < chips)
    far_id = (jnp.clip(far, 0, chips - 1), mate)
    mate_id = (space, mate)
    long = has_far & ((space + core) % ROW == 0)
    short = has_far & jnp.logical_not(long)
    early = long | (has_far & ((space + core) % 4 == 0)) | (me == 1)
    first = long & (core == 0) & (space % 32 == 0) & (space % 128 != 0)
    second = long & (core == 1)
    fsurf = (fx, fy, fz)
    esurf = (ex, ey, ez)
    hsurf = (hx, hy, hz)
    sums = (px, py, pz)
    far_sums = (qx, qy, qz)
    given_sums = (gx, gy, gz)

    barrier = pltpu.get_barrier_semaphore()
    pl.semaphore_signal(barrier, inc=1, device_id=mate_id, device_id_type=MESH)

    @pl.when(has_far)
    def _():
        pl.semaphore_signal(barrier, inc=1, device_id=far_id, device_id_type=MESH)

    local = [
        pltpu.make_async_copy(feat, own, lsem.at[0]),
        pltpu.make_async_copy(nbr, tab, lsem.at[1]),
        pltpu.make_async_copy(occ, occs, lsem.at[2]),
        pltpu.make_async_copy(wk1, stage1, lsem.at[3]),
        pltpu.make_async_copy(wk2, stage2, lsem.at[4]),
    ]
    for copy in local:
        copy.start()

    for surf in fsurf + esurf + hsurf:
        surf[0] = jnp.zeros((64, 2 * C), BF16)

    def unpack(stage, weights, h, i):
        for jk in range(9):
            tile = stage[i, jk // 3, jk % 3]
            weights[h, 9 * i + jk, 0:48, :] = tile[:, 0:C]
            weights[h, 9 * i + jk, 48:96, :] = tile[:, C:2 * C]

    def remote(source, target, send, recv, device):
        return pltpu.make_async_remote_copy(
            src_ref=source, dst_ref=target, send_sem=send, recv_sem=recv,
            device_id=device, device_id_type=MESH)

    def sends(surf, sems, recvs, axis):
        return (
            remote(surf[axis].at[2], surf[axis].at[1], sems.at[0, axis], recvs.at[0, axis], mate_id),
            remote(surf[axis].at[2], surf[axis].at[3], sems.at[1, axis], recvs.at[1, axis], far_id),
        )

    fcopies = [sends(fsurf, fsend, frecv, axis) for axis in range(3)]
    hcopies = [sends(hsurf, hsend, hrecv, axis) for axis in range(3)]
    ecopies = [
        remote(fsurf[axis].at[2], esurf[axis].at[1], fsend.at[1, axis], frecv.at[1, axis], far_id)
        for axis in range(3)]
    pcopies = [
        remote(sums[axis], far_sums[axis], psend.at[axis], precv.at[axis], far_id) for axis in range(3)]
    tcopy = remote(nbr, ftab, psend.at[3], precv.at[3], far_id)

    order = (1, 0, 2)
    wcopies = [
        remote(wk1.at[i], mate1.at[i], wsend.at[n], wrecv.at[n], mate_id) for n, i in enumerate(order)]
    for n, i in enumerate(order):
        part = w2.at[core, pl.ds(9 * i, 9)]
        wcopies.append(remote(part, part, wsend.at[3 + n], wrecv.at[3 + n], mate_id))

    def prepare_faces():
        local[0].wait()
        for x in range(8):
            put(acc, slice(64 * x, 64 * x + 64), own[x].astype(F32))
        for axis in range(3):
            pack_pair(fsurf[axis].at[2], acc, lambda v: v.astype(BF16), axis)

    def prepare_own():
        for x in range(8):
            own_columns(cols.at[x], own[x])
        local[3].wait()
        for i in order:
            unpack(stage1, w1, core, i)

    def unpack_two():
        local[4].wait()
        for i in order:
            unpack(stage2, w2, core, i)

    def send_two():
        for n in range(3):
            wcopies[3 + n].start()

    def own_part(with_two=True, send=True):
        if with_two:
            local[4].wait()
        for n, i in enumerate(order):
            wcopies[n].wait_recv()
            unpack(mate1, w1, mate, i)
            if with_two:
                unpack(stage2, w2, core, i)
            for start, stop in (((1, 4), (4, 8)), ((0, 4), (4, 8)), ((0, 4), (4, 7)))[i]:
                rows = slice(64 * start, 64 * stop)
                d = own_product(cols, w1, i, start, stop)
                put(acc, rows, get(acc, rows) + d if n else d)
            if send:
                wcopies[3 + n].start()

    @pl.when(early)
    def _():
        prepare_faces()
        prepare_own()

    pl.when(first)(functools.partial(own_part, True, False))
    pl.semaphore_wait(barrier, 1 + has_far.astype(jnp.int32))

    @pl.when(jnp.logical_not(early))
    def _():
        for n in range(3):
            wcopies[n].start()
        prepare_faces()

    pl.when(long)(tcopy.start)
    for axis in range(3):
        pl.when(short)(fcopies[axis][1].start)
        pl.when(long)(ecopies[axis].start)
        fcopies[axis][0].start()

    @pl.when(early)
    def _():
        for n in range(3):
            wcopies[n].start()

    pl.when(jnp.logical_not(early))(prepare_own)

    local[1].wait()
    local[2].wait()
    where = []
    for t in range(27):
        n = tab[0, t]
        where.append(jnp.where(n < 0, 0, jnp.where(n == me, 2, jnp.where(n == mate_slot, 1, 3))))
    active = occs[0].astype(F32)

    pl.when(jnp.logical_not(first | second))(own_part)
    pl.when(second)(functools.partial(own_part, False, False))
    pl.when(first)(send_two)

    @pl.when(jnp.logical_not(long))
    def _():
        def arrived(axis):
            fcopies[axis][0].wait_recv()
            pl.when(short)(fcopies[axis][1].wait_recv)

        add_faces(acc, fcols, fsurf, where, w1, arrived)

    @pl.when(long)
    def _():
        near = [jnp.where(w == 3, 0, w) for w in where]
        add_faces(acc, fcols, fsurf, near, w1, lambda axis: fcopies[axis][0].wait_recv())
        for axis in range(3):
            pack_pair(sums[axis], acc, lambda v: v.astype(BF16), axis)
            pcopies[axis].start()

        @pl.when(second)
        def _():
            unpack_two()
            send_two()

        tcopy.wait_recv()
        fetch = pltpu.make_async_copy(ftab, tab2, lsem.at[5])
        fetch.start()
        facc[...] = jnp.zeros((2, 512, 128), F32)
        fetch.wait()
        given = [jnp.where(tab2[0, t] == me, 2, 0) for t in range(27)]
        add_faces(facc, fcols, fsurf, given, w1, lambda axis: None)
        for axis in range(3):
            pack_pair(given_sums[axis], facc, lambda v: v, axis)
        away = [jnp.where(w == 3, 1, 0) for w in where]
        add_faces(acc, fcols, esurf, away, w1, lambda axis: ecopies[axis].wait_recv())

    def hidden(v):
        return (jnp.maximum(v, 0.0) * active).astype(BF16)

    for axis in range(3):
        pack_pair(hsurf[axis].at[2], acc, hidden, axis)
        pl.when(short)(hcopies[axis][1].start)
        hcopies[axis][0].start()

    for n in range(3):
        wcopies[3 + n].wait_recv()
    for x in range(8):
        own_columns(cols.at[x], hidden(get(acc, slice(64 * x, 64 * x + 64))))
    res = own[0:4].reshape(256, C).astype(F32)
    d = own_product(cols, w2, 1, 0, 4) + own_product(cols, w2, 2, 0, 4) + res
    put(acc2, slice(0, 64), d[:64])
    put(acc2, slice(64, 256), d[64:] + own_product(cols, w2, 0, 1, 4))
    res = own[4:8].reshape(256, C).astype(F32)
    d = own_product(cols, w2, 1, 4, 8) + own_product(cols, w2, 0, 4, 8) + res
    put(acc2, slice(256, 448), d[:192] + own_product(cols, w2, 2, 4, 7))
    put(acc2, slice(448, 512), d[192:])
    act[...] = jnp.full((8, C), active, F32)

    for copy in wcopies:
        copy.wait_send()
    for axis in range(3):
        fcopies[axis][0].wait_send()
        pl.when(short)(fcopies[axis][1].wait_send)
        pl.when(long)(ecopies[axis].wait_send)

    @pl.when(long)
    def _():
        tcopy.wait_send()
        for axis in range(3):
            pcopies[axis].wait_send()

    def arrived(axis):
        hcopies[axis][0].wait_recv()
        pl.when(short)(hcopies[axis][1].wait_recv)

        @pl.when(long)
        def _():
            pcopies[axis].wait_recv()
            hsurf[axis][3] = jnp.maximum(
                far_sums[axis][...].astype(F32) + given_sums[axis][...], 0.0).astype(BF16)

    add_faces(acc2, fcols, hsurf, where, w2, arrived)
    for near, away in hcopies:
        near.wait_send()
        pl.when(short)(away.wait_send)


def finish_kernel(acc2, act, out, done, sem):
    scale = act[0:1, :]
    copies = []
    for part in range(4):
        for x in (2 * part, 2 * part + 1):
            done[x] = jnp.maximum(get(acc2, slice(64 * x, 64 * x + 64)), 0.0) * scale
        rows = pl.ds(2 * part, 2)
        copies.append(pltpu.make_async_copy(done.at[rows], out.at[rows], sem.at[part]))
        copies[part].start()
    for copy in copies:
        copy.wait()


def body(features, occupancy, neighbours, kernel_one, kernel_two):
    total = lax.axis_size("space") * lax.axis_size("wt")
    hbm = pl.BlockSpec(memory_space=pltpu.HBM)
    vmem = pl.BlockSpec(memory_space=pltpu.VMEM)

    def pinned(v):
        return pltpu.with_memory_space_constraint(v, pltpu.HBM)

    middle = pl.pallas_call(
        functools.partial(exchange_kernel, total),
        out_shape=(
            pltpu.VMEM((2, 512, 128), F32),
            pltpu.VMEM((8, C), F32),
        ),
        in_specs=[hbm] * 5,
        out_specs=(vmem,) * 2,
        scratch_shapes=[
            pltpu.VMEM((8, 64, C), BF16),
            *[pltpu.VMEM((4, 64, 2 * C), BF16)] * 3,
            *[pltpu.VMEM((2, 64, 2 * C), BF16)] * 3,
            *[pltpu.VMEM((4, 64, 2 * C), BF16)] * 3,
            *[pltpu.VMEM((3, 3, 3, 48, 2 * C), BF16)] * 3,
            pltpu.VMEM((2, 27, 96, C), BF16),
            pltpu.VMEM((2, 27, 96, C), BF16),
            pltpu.VMEM((8, 64, 9 * C), BF16),
            pltpu.VMEM((6, 64, 9 * C), BF16),
            pltpu.VMEM((2, 512, 128), F32),
            pltpu.VMEM((2, 512, 128), F32),
            *[pltpu.VMEM((64, 2 * C), BF16)] * 6,
            *[pltpu.VMEM((64, 2 * C), F32)] * 3,
            pltpu.VMEM((1, 27), jnp.int32),
            pltpu.SMEM((1, 27), jnp.int32),
            pltpu.SMEM((1, 27), jnp.int32),
            pltpu.SMEM((1,), jnp.int32),
            pltpu.SemaphoreType.DMA((6,)),
            pltpu.SemaphoreType.DMA((2, 3)),
            pltpu.SemaphoreType.DMA((2, 3)),
            pltpu.SemaphoreType.DMA((6,)),
            pltpu.SemaphoreType.DMA((6,)),
            pltpu.SemaphoreType.DMA((2, 3)),
            pltpu.SemaphoreType.DMA((2, 3)),
            pltpu.SemaphoreType.DMA((4,)),
            pltpu.SemaphoreType.DMA((4,)),
        ],
        compiler_params=pltpu.CompilerParams(
            collective_id=0, has_side_effects=True, vmem_limit_bytes=32 * 1024 * 1024),
    )(pinned(features.reshape(8, 64, C)), occupancy, pinned(neighbours), pinned(kernel_one), pinned(kernel_two))
    y = pl.pallas_call(
        finish_kernel,
        out_shape=jax.ShapeDtypeStruct((8, 64, C), F32),
        in_specs=[vmem] * 2,
        out_specs=hbm,
        scratch_shapes=[pltpu.VMEM((8, 64, C), F32), pltpu.SemaphoreType.DMA((4,))],
        compiler_params=pltpu.CompilerParams(vmem_limit_bytes=16 * 1024 * 1024),
    )(*middle)
    return y.reshape(1, 8, 8, 8, C)


def solution(mesh):
    return jax.shard_map(
        body,
        mesh=mesh,
        in_specs=(
            P(("space", "wt"), None, None, None, None),
            P(("space", "wt")),
            P(("space", "wt"), None),
            P(None, None, None, None, "wt"),
            P(None, None, None, None, "wt"),
        ),
        out_specs=P(("space", "wt"), None, None, None, None),
        check_vma=False,
    )
```

```python
import functools

import jax
import jax.numpy as jnp
from jax import lax
from jax.experimental import pallas as pl
from jax.experimental.pallas import tpu as pltpu
from jax.sharding import PartitionSpec as P

C = 192
MESH = pl.DeviceIdType.MESH
F32 = jnp.float32
BF16 = jnp.bfloat16
ROW = 16
FACES = ((-1, 0, 0), (1, 0, 0), (0, -1, 0), (0, 1, 0), (0, 0, -1), (0, 0, 1))


def columns(dst, low, mid, high):
    row = lax.broadcasted_iota(jnp.int32, (80, C), 0) % 8
    lo = jnp.where(row == 7, low, mid).reshape(10, 8, C)
    hi = jnp.where(row == 0, high, mid).reshape(10, 8, C)
    shifted = (pltpu.roll(lo, 1, 1).reshape(80, C), mid, pltpu.roll(hi, 7, 1).reshape(80, C))
    for inner in range(3):
        for outer in range(3):
            at = (3 * outer + inner) * C
            dst[:, at:at + C] = shifted[inner][8 * outer:8 * outer + 64].astype(BF16)


def framed(value):
    edge = jnp.zeros((8, C), F32)
    return jnp.concatenate([edge, value, edge], axis=0)


def own_columns(dst, value):
    columns(dst, 0.0, framed(value.astype(F32)), 0.0)


def taps(weights, chosen):
    return jnp.concatenate([weights[h, t] for t in chosen for h in range(2)], axis=0)


def own_product(cols, weights, i, first, last):
    lhs = cols[first + i - 1:last + i - 1].reshape(64 * (last - first), 9 * C)
    return jnp.dot(lhs, taps(weights, range(9 * i, 9 * i + 9)), preferred_element_type=F32)


def face_columns(dst, surf, where, n):
    a, b, c = FACES[n]

    def face(p, q, r):
        pair = surf[where[9 * (p + 1) + 3 * (q + 1) + (r + 1)]]
        return (pair[:, C:] if a + b + c < 0 else pair[:, :C]).astype(F32)

    if a:
        def line(r):
            return jnp.concatenate([face(a, -1, r)[56:64], face(a, 0, r), face(a, 1, r)[0:8]], axis=0)
        columns(dst.at[n], line(-1), line(0), line(1))
    elif b:
        columns(dst.at[n], *(framed(face(0, b, r)) for r in (-1, 0, 1)))
    else:
        columns(dst.at[n], 0.0, framed(face(0, 0, c)), 0.0)


def face_product(fcols, weights, n):
    a, b, c = FACES[n]
    if a:
        chosen = [9 * (a + 1) + t for t in range(9)]
    elif b:
        chosen = [9 * i + 3 * (b + 1) + k for i in range(3) for k in range(3)]
    else:
        chosen = [9 * i + 3 * j + c + 1 for i in range(3) for j in range(3)]
    return jnp.dot(fcols[n], taps(weights, chosen), preferred_element_type=F32)


def put(acc, rows, value):
    acc[0, rows, :] = value[:, :128]
    acc[1, rows, 0:C - 128] = value[:, 128:]


def get(acc, rows):
    return jnp.concatenate([acc[0, rows, :], acc[1, rows, 0:C - 128]], axis=1)


def add_pair(acc, fcols, weights, axis):
    for n in (2 * axis, 2 * axis + 1):
        a, b, c = FACES[n]
        d = face_product(fcols, weights, n)
        if a:
            rows = slice(0, 64) if a < 0 else slice(448, 512)
            put(acc, rows, get(acc, rows) + d)
        elif b:
            first = 0 if b < 0 else 56
            for x in range(8):
                rows = slice(64 * x + first, 64 * x + first + 8)
                put(acc, rows, get(acc, rows) + d[8 * x:8 * x + 8])
        else:
            rows = pl.ds(0 if c < 0 else 7, 64, stride=8)
            rest = jnp.concatenate([d[:, 128:], jnp.zeros((64, 256 - C), F32)], axis=1)
            for part, value in enumerate((d[:, :128], rest)):
                acc[part, rows, :] = acc[part, rows, :] + value


def add_faces(acc, fcols, surf, where, weights, arrived):
    for axis in range(3):
        arrived(axis)
        if axis:
            add_pair(acc, fcols, weights, axis - 1)
        for n in (2 * axis, 2 * axis + 1):
            face_columns(fcols, surf[axis], where, n)
    add_pair(acc, fcols, weights, 2)


def pack_pair(dst, field, fix, axis):
    def rows_of(side):
        if axis == 0:
            return get(field, slice(448 * side, 448 * side + 64))
        if axis == 1:
            return jnp.concatenate(
                [get(field, slice(64 * x + 56 * side, 64 * x + 56 * side + 8)) for x in range(8)], axis=0)
        rows = pl.ds(7 * side, 64, stride=8)
        return jnp.concatenate([field[0, rows, :], field[1, rows, :][:, 0:C - 128]], axis=1)

    dst[:, :C] = fix(rows_of(0))
    dst[:, C:] = fix(rows_of(1))


def exchange_kernel(
    total, feat, occ, nbr, wk1, wk2,
    acc2, act,
    own, fx, fy, fz, ex, ey, ez, hx, hy, hz, stage1, mate1, stage2, mate2, w1, w2, cols, fcols, acc, facc,
    px, py, pz, qx, qy, qz, gx, gy, gz, ftab, tab, tab2, occs,
    lsem, fsend, frecv, wsend, wrecv, hsend, hrecv, psend, precv,
):
    space = lax.axis_index("space")
    core = lax.axis_index("wt")
    chips = total // 2
    me = space * 2 + core
    mate = 1 - core
    mate_slot = space * 2 + mate
    step = 2 * core - 1
    far = space + step
    has_far = (far >= 0) & (far < chips)
    far_id = (jnp.clip(far, 0, chips - 1), mate)
    mate_id = (space, mate)
    long = has_far & ((space + core) % ROW == 0)
    short = has_far & jnp.logical_not(long)
    early = long | (has_far & ((space + core) % 4 == 0)) | (me == 1)
    first = long & (core == 0) & (space % 32 == 0) & (space % 128 != 0)
    second = long & (core == 1)
    raw = me == 0
    ready = me == 1
    fsurf = (fx, fy, fz)
    esurf = (ex, ey, ez)
    hsurf = (hx, hy, hz)
    sums = (px, py, pz)
    far_sums = (qx, qy, qz)
    given_sums = (gx, gy, gz)

    barrier = pltpu.get_barrier_semaphore()
    pl.semaphore_signal(barrier, inc=1, device_id=mate_id, device_id_type=MESH)

    @pl.when(has_far)
    def _():
        pl.semaphore_signal(barrier, inc=1, device_id=far_id, device_id_type=MESH)

    local = [
        pltpu.make_async_copy(feat, own, lsem.at[0]),
        pltpu.make_async_copy(nbr, tab, lsem.at[1]),
        pltpu.make_async_copy(occ, occs, lsem.at[2]),
        pltpu.make_async_copy(wk1, stage1, lsem.at[3]),
        pltpu.make_async_copy(wk2, stage2, lsem.at[4]),
    ]
    for copy in local:
        copy.start()

    for surf in fsurf + esurf + hsurf:
        surf[0] = jnp.zeros((64, 2 * C), BF16)

    def unpack(stage, weights, h, i):
        for jk in range(9):
            tile = stage[i, jk // 3, jk % 3]
            weights[h, 9 * i + jk, 0:48, :] = tile[:, 0:C]
            weights[h, 9 * i + jk, 48:96, :] = tile[:, C:2 * C]

    def remote(source, target, send, recv, device):
        return pltpu.make_async_remote_copy(
            src_ref=source, dst_ref=target, send_sem=send, recv_sem=recv,
            device_id=device, device_id_type=MESH)

    def sends(surf, sems, recvs, axis):
        return (
            remote(surf[axis].at[2], surf[axis].at[1], sems.at[0, axis], recvs.at[0, axis], mate_id),
            remote(surf[axis].at[2], surf[axis].at[3], sems.at[1, axis], recvs.at[1, axis], far_id),
        )

    fcopies = [sends(fsurf, fsend, frecv, axis) for axis in range(3)]
    hcopies = [sends(hsurf, hsend, hrecv, axis) for axis in range(3)]
    ecopies = [
        remote(fsurf[axis].at[2], esurf[axis].at[1], fsend.at[1, axis], frecv.at[1, axis], far_id)
        for axis in range(3)]
    pcopies = [
        remote(sums[axis], far_sums[axis], psend.at[axis], precv.at[axis], far_id) for axis in range(3)]
    tcopy = remote(nbr, ftab, psend.at[3], precv.at[3], far_id)

    order = (1, 0, 2)
    wcopies = [
        remote(wk1.at[i], mate1.at[i], wsend.at[n], wrecv.at[n], mate_id) for n, i in enumerate(order)]
    for n, i in enumerate(order):
        part = w2.at[core, pl.ds(9 * i, 9)]
        wcopies.append(remote(part, part, wsend.at[3 + n], wrecv.at[3 + n], mate_id))

    rcopies = [
        remote(wk2.at[i], mate2.at[i], wsend.at[3 + n], wrecv.at[3 + n], mate_id)
        for n, i in enumerate(order)]

    def start_raw():
        for copy in rcopies:
            copy.start()

    def prepare_faces():
        local[0].wait()
        for x in range(8):
            put(acc, slice(64 * x, 64 * x + 64), own[x].astype(F32))
        for axis in range(3):
            pack_pair(fsurf[axis].at[2], acc, lambda v: v.astype(BF16), axis)

    def prepare_own():
        for x in range(8):
            own_columns(cols.at[x], own[x])
        local[3].wait()
        for i in order:
            unpack(stage1, w1, core, i)

    def unpack_two():
        local[4].wait()
        for i in order:
            unpack(stage2, w2, core, i)

    def send_two():
        for n in range(3):
            wcopies[3 + n].start()

    def own_part(with_two=True, send=True):
        if with_two:
            local[4].wait()
        for n, i in enumerate(order):
            wcopies[n].wait_recv()
            unpack(mate1, w1, mate, i)
            if with_two:
                unpack(stage2, w2, core, i)
            for start, stop in (((1, 4), (4, 8)), ((0, 4), (4, 8)), ((0, 4), (4, 7)))[i]:
                rows = slice(64 * start, 64 * stop)
                d = own_product(cols, w1, i, start, stop)
                put(acc, rows, get(acc, rows) + d if n else d)
            if send:
                wcopies[3 + n].start()

    @pl.when(early)
    def _():
        prepare_faces()
        prepare_own()

    pl.when(ready)(unpack_two)
    pl.when(first)(functools.partial(own_part, True, False))
    pl.semaphore_wait(barrier, 1 + has_far.astype(jnp.int32))

    @pl.when(jnp.logical_not(early))
    def _():
        for n in range(3):
            wcopies[n].start()
        pl.when(raw)(start_raw)
        prepare_faces()

    pl.when(long)(tcopy.start)
    for axis in range(3):
        pl.when(short)(fcopies[axis][1].start)
        pl.when(long)(ecopies[axis].start)
        fcopies[axis][0].start()

    @pl.when(early)
    def _():
        for n in range(3):
            wcopies[n].start()

    pl.when(ready)(send_two)
    pl.when(jnp.logical_not(early))(prepare_own)

    local[1].wait()
    local[2].wait()
    where = []
    for t in range(27):
        n = tab[0, t]
        where.append(jnp.where(n < 0, 0, jnp.where(n == me, 2, jnp.where(n == mate_slot, 1, 3))))
    active = occs[0].astype(F32)

    pl.when(jnp.logical_not(first | second | ready | raw))(own_part)
    pl.when(second | ready | raw)(functools.partial(own_part, False, False))
    pl.when(first)(send_two)

    @pl.when(jnp.logical_not(long))
    def _():
        def arrived(axis):
            fcopies[axis][0].wait_recv()
            pl.when(short)(fcopies[axis][1].wait_recv)

        add_faces(acc, fcols, fsurf, where, w1, arrived)

    @pl.when(long)
    def _():
        near = [jnp.where(w == 3, 0, w) for w in where]
        add_faces(acc, fcols, fsurf, near, w1, lambda axis: fcopies[axis][0].wait_recv())
        for axis in range(3):
            pack_pair(sums[axis], acc, lambda v: v.astype(BF16), axis)
            pcopies[axis].start()

        @pl.when(second)
        def _():
            unpack_two()
            send_two()

        tcopy.wait_recv()
        fetch = pltpu.make_async_copy(ftab, tab2, lsem.at[5])
        fetch.start()
        facc[...] = jnp.zeros((2, 512, 128), F32)
        fetch.wait()
        given = [jnp.where(tab2[0, t] == me, 2, 0) for t in range(27)]
        add_faces(facc, fcols, fsurf, given, w1, lambda axis: None)
        for axis in range(3):
            pack_pair(given_sums[axis], facc, lambda v: v, axis)
        away = [jnp.where(w == 3, 1, 0) for w in where]
        add_faces(acc, fcols, esurf, away, w1, lambda axis: ecopies[axis].wait_recv())

    def hidden(v):
        return (jnp.maximum(v, 0.0) * active).astype(BF16)

    for axis in range(3):
        pack_pair(hsurf[axis].at[2], acc, hidden, axis)
        pl.when(short)(hcopies[axis][1].start)
        hcopies[axis][0].start()

    pl.when(raw)(unpack_two)

    @pl.when(ready)
    def _():
        for n, i in enumerate(order):
            rcopies[n].wait_recv()
            unpack(mate2, w2, mate, i)

    @pl.when(jnp.logical_not(ready))
    def _():
        for n in range(3):
            wcopies[3 + n].wait_recv()

    for x in range(8):
        own_columns(cols.at[x], hidden(get(acc, slice(64 * x, 64 * x + 64))))
    res = own[0:4].reshape(256, C).astype(F32)
    d = own_product(cols, w2, 1, 0, 4) + own_product(cols, w2, 2, 0, 4) + res
    put(acc2, slice(0, 64), d[:64])
    put(acc2, slice(64, 256), d[64:] + own_product(cols, w2, 0, 1, 4))
    res = own[4:8].reshape(256, C).astype(F32)
    d = own_product(cols, w2, 1, 4, 8) + own_product(cols, w2, 0, 4, 8) + res
    put(acc2, slice(256, 448), d[:192] + own_product(cols, w2, 2, 4, 7))
    put(acc2, slice(448, 512), d[192:])
    act[...] = jnp.full((8, C), active, F32)

    for n in range(3):
        wcopies[n].wait_send()
        pl.when(raw)(rcopies[n].wait_send)
        pl.when(jnp.logical_not(raw))(wcopies[3 + n].wait_send)
    for axis in range(3):
        fcopies[axis][0].wait_send()
        pl.when(short)(fcopies[axis][1].wait_send)
        pl.when(long)(ecopies[axis].wait_send)

    @pl.when(long)
    def _():
        tcopy.wait_send()
        for axis in range(3):
            pcopies[axis].wait_send()

    def arrived(axis):
        hcopies[axis][0].wait_recv()
        pl.when(short)(hcopies[axis][1].wait_recv)

        @pl.when(long)
        def _():
            pcopies[axis].wait_recv()
            hsurf[axis][3] = jnp.maximum(
                far_sums[axis][...].astype(F32) + given_sums[axis][...], 0.0).astype(BF16)

    add_faces(acc2, fcols, hsurf, where, w2, arrived)
    for near, away in hcopies:
        near.wait_send()
        pl.when(short)(away.wait_send)


def finish_kernel(acc2, act, out, done, sem):
    scale = act[0:1, :]
    copies = []
    for part in range(4):
        for x in (2 * part, 2 * part + 1):
            done[x] = jnp.maximum(get(acc2, slice(64 * x, 64 * x + 64)), 0.0) * scale
        rows = pl.ds(2 * part, 2)
        copies.append(pltpu.make_async_copy(done.at[rows], out.at[rows], sem.at[part]))
        copies[part].start()
    for copy in copies:
        copy.wait()


def body(features, occupancy, neighbours, kernel_one, kernel_two):
    total = lax.axis_size("space") * lax.axis_size("wt")
    hbm = pl.BlockSpec(memory_space=pltpu.HBM)
    vmem = pl.BlockSpec(memory_space=pltpu.VMEM)

    def pinned(v):
        return pltpu.with_memory_space_constraint(v, pltpu.HBM)

    middle = pl.pallas_call(
        functools.partial(exchange_kernel, total),
        out_shape=(
            pltpu.VMEM((2, 512, 128), F32),
            pltpu.VMEM((8, C), F32),
        ),
        in_specs=[hbm] * 5,
        out_specs=(vmem,) * 2,
        scratch_shapes=[
            pltpu.VMEM((8, 64, C), BF16),
            *[pltpu.VMEM((4, 64, 2 * C), BF16)] * 3,
            *[pltpu.VMEM((2, 64, 2 * C), BF16)] * 3,
            *[pltpu.VMEM((4, 64, 2 * C), BF16)] * 3,
            *[pltpu.VMEM((3, 3, 3, 48, 2 * C), BF16)] * 4,
            pltpu.VMEM((2, 27, 96, C), BF16),
            pltpu.VMEM((2, 27, 96, C), BF16),
            pltpu.VMEM((8, 64, 9 * C), BF16),
            pltpu.VMEM((6, 64, 9 * C), BF16),
            pltpu.VMEM((2, 512, 128), F32),
            pltpu.VMEM((2, 512, 128), F32),
            *[pltpu.VMEM((64, 2 * C), BF16)] * 6,
            *[pltpu.VMEM((64, 2 * C), F32)] * 3,
            pltpu.VMEM((1, 27), jnp.int32),
            pltpu.SMEM((1, 27), jnp.int32),
            pltpu.SMEM((1, 27), jnp.int32),
            pltpu.SMEM((1,), jnp.int32),
            pltpu.SemaphoreType.DMA((6,)),
            pltpu.SemaphoreType.DMA((2, 3)),
            pltpu.SemaphoreType.DMA((2, 3)),
            pltpu.SemaphoreType.DMA((6,)),
            pltpu.SemaphoreType.DMA((6,)),
            pltpu.SemaphoreType.DMA((2, 3)),
            pltpu.SemaphoreType.DMA((2, 3)),
            pltpu.SemaphoreType.DMA((4,)),
            pltpu.SemaphoreType.DMA((4,)),
        ],
        compiler_params=pltpu.CompilerParams(
            collective_id=0, has_side_effects=True, vmem_limit_bytes=32 * 1024 * 1024),
    )(pinned(features.reshape(8, 64, C)), occupancy, pinned(neighbours), pinned(kernel_one), pinned(kernel_two))
    y = pl.pallas_call(
        finish_kernel,
        out_shape=jax.ShapeDtypeStruct((8, 64, C), F32),
        in_specs=[vmem] * 2,
        out_specs=hbm,
        scratch_shapes=[pltpu.VMEM((8, 64, C), F32), pltpu.SemaphoreType.DMA((4,))],
        compiler_params=pltpu.CompilerParams(vmem_limit_bytes=16 * 1024 * 1024),
    )(*middle)
    return y.reshape(1, 8, 8, 8, C)


def solution(mesh):
    return jax.shard_map(
        body,
        mesh=mesh,
        in_specs=(
            P(("space", "wt"), None, None, None, None),
            P(("space", "wt")),
            P(("space", "wt"), None),
            P(None, None, None, None, "wt"),
            P(None, None, None, None, "wt"),
        ),
        out_specs=P(("space", "wt"), None, None, None, None),
        check_vma=False,
    )
```

```python
import functools

import jax
import jax.numpy as jnp
from jax import lax
from jax.experimental import pallas as pl
from jax.experimental.pallas import tpu as pltpu
from jax.sharding import PartitionSpec as P

C = 192
MESH = pl.DeviceIdType.MESH
F32 = jnp.float32
BF16 = jnp.bfloat16
ROW = 16
FACES = ((-1, 0, 0), (1, 0, 0), (0, -1, 0), (0, 1, 0), (0, 0, -1), (0, 0, 1))


def columns(dst, low, mid, high):
    row = lax.broadcasted_iota(jnp.int32, (80, C), 0) % 8
    lo = jnp.where(row == 7, low, mid).reshape(10, 8, C)
    hi = jnp.where(row == 0, high, mid).reshape(10, 8, C)
    shifted = (pltpu.roll(lo, 1, 1).reshape(80, C), mid, pltpu.roll(hi, 7, 1).reshape(80, C))
    for inner in range(3):
        for outer in range(3):
            at = (3 * outer + inner) * C
            dst[:, at:at + C] = shifted[inner][8 * outer:8 * outer + 64].astype(BF16)


def framed(value):
    edge = jnp.zeros((8, C), F32)
    return jnp.concatenate([edge, value, edge], axis=0)


def own_columns(dst, value):
    columns(dst, 0.0, framed(value.astype(F32)), 0.0)


def taps(weights, chosen):
    return jnp.concatenate([weights[h, t] for t in chosen for h in range(2)], axis=0)


def own_product(cols, weights, i, first, last):
    lhs = cols[first + i - 1:last + i - 1].reshape(64 * (last - first), 9 * C)
    return jnp.dot(lhs, taps(weights, range(9 * i, 9 * i + 9)), preferred_element_type=F32)


def face_columns(dst, surf, where, n):
    a, b, c = FACES[n]

    def face(p, q, r):
        pair = surf[where[9 * (p + 1) + 3 * (q + 1) + (r + 1)]]
        return (pair[:, C:] if a + b + c < 0 else pair[:, :C]).astype(F32)

    if a:
        def line(r):
            return jnp.concatenate([face(a, -1, r)[56:64], face(a, 0, r), face(a, 1, r)[0:8]], axis=0)
        columns(dst.at[n], line(-1), line(0), line(1))
    elif b:
        columns(dst.at[n], *(framed(face(0, b, r)) for r in (-1, 0, 1)))
    else:
        columns(dst.at[n], 0.0, framed(face(0, 0, c)), 0.0)


def face_product(fcols, weights, n):
    a, b, c = FACES[n]
    if a:
        chosen = [9 * (a + 1) + t for t in range(9)]
    elif b:
        chosen = [9 * i + 3 * (b + 1) + k for i in range(3) for k in range(3)]
    else:
        chosen = [9 * i + 3 * j + c + 1 for i in range(3) for j in range(3)]
    return jnp.dot(fcols[n], taps(weights, chosen), preferred_element_type=F32)


def put(acc, rows, value):
    acc[0, rows, :] = value[:, :128]
    acc[1, rows, 0:C - 128] = value[:, 128:]


def get(acc, rows):
    return jnp.concatenate([acc[0, rows, :], acc[1, rows, 0:C - 128]], axis=1)


def add_pair(acc, fcols, weights, axis):
    for n in (2 * axis, 2 * axis + 1):
        a, b, c = FACES[n]
        d = face_product(fcols, weights, n)
        if a:
            rows = slice(0, 64) if a < 0 else slice(448, 512)
            put(acc, rows, get(acc, rows) + d)
        elif b:
            first = 0 if b < 0 else 56
            for x in range(8):
                rows = slice(64 * x + first, 64 * x + first + 8)
                put(acc, rows, get(acc, rows) + d[8 * x:8 * x + 8])
        else:
            rows = pl.ds(0 if c < 0 else 7, 64, stride=8)
            rest = jnp.concatenate([d[:, 128:], jnp.zeros((64, 256 - C), F32)], axis=1)
            for part, value in enumerate((d[:, :128], rest)):
                acc[part, rows, :] = acc[part, rows, :] + value


def add_faces(acc, fcols, surf, where, weights, arrived):
    for axis in range(3):
        arrived(axis)
        if axis:
            add_pair(acc, fcols, weights, axis - 1)
        for n in (2 * axis, 2 * axis + 1):
            face_columns(fcols, surf[axis], where, n)
    add_pair(acc, fcols, weights, 2)


def pack_pair(dst, field, fix, axis):
    def rows_of(side):
        if axis == 0:
            return get(field, slice(448 * side, 448 * side + 64))
        if axis == 1:
            return jnp.concatenate(
                [get(field, slice(64 * x + 56 * side, 64 * x + 56 * side + 8)) for x in range(8)], axis=0)
        rows = pl.ds(7 * side, 64, stride=8)
        return jnp.concatenate([field[0, rows, :], field[1, rows, :][:, 0:C - 128]], axis=1)

    dst[:, :C] = fix(rows_of(0))
    dst[:, C:] = fix(rows_of(1))


def exchange_kernel(
    total, feat, occ, nbr, wk1, wk2,
    acc2, act,
    own, fx, fy, fz, ex, ey, ez, hx, hy, hz, stage1, mate1, stage2, w1, w2, cols, fcols, acc, facc,
    px, py, pz, qx, qy, qz, gx, gy, gz, ftab, tab, tab2, occs,
    lsem, fsend, frecv, wsend, wrecv, hsend, hrecv, psend, precv,
):
    space = lax.axis_index("space")
    core = lax.axis_index("wt")
    chips = total // 2
    me = space * 2 + core
    mate = 1 - core
    mate_slot = space * 2 + mate
    step = 2 * core - 1
    far = space + step
    has_far = (far >= 0) & (far < chips)
    far_id = (jnp.clip(far, 0, chips - 1), mate)
    mate_id = (space, mate)
    long = has_far & ((space + core) % ROW == 0)
    short = has_far & jnp.logical_not(long)
    early = long | (has_far & ((space + core) % 4 == 0)) | (me == 1)
    first = long & (core == 0) & (space % 32 == 0) & (space % 128 != 0)
    second = long & (core == 1)
    fsurf = (fx, fy, fz)
    esurf = (ex, ey, ez)
    hsurf = (hx, hy, hz)
    sums = (px, py, pz)
    far_sums = (qx, qy, qz)
    given_sums = (gx, gy, gz)

    barrier = pltpu.get_barrier_semaphore()
    pl.semaphore_signal(barrier, inc=1, device_id=mate_id, device_id_type=MESH)

    @pl.when(has_far)
    def _():
        pl.semaphore_signal(barrier, inc=1, device_id=far_id, device_id_type=MESH)

    local = [
        pltpu.make_async_copy(feat, own, lsem.at[0]),
        pltpu.make_async_copy(nbr, tab, lsem.at[1]),
        pltpu.make_async_copy(occ, occs, lsem.at[2]),
        pltpu.make_async_copy(wk1, stage1, lsem.at[3]),
        pltpu.make_async_copy(wk2, stage2, lsem.at[4]),
    ]
    for copy in local:
        copy.start()

    for surf in fsurf + esurf + hsurf:
        surf[0] = jnp.zeros((64, 2 * C), BF16)

    def unpack(stage, weights, h, i):
        for jk in range(9):
            tile = stage[i, jk // 3, jk % 3]
            weights[h, 9 * i + jk, 0:48, :] = tile[:, 0:C]
            weights[h, 9 * i + jk, 48:96, :] = tile[:, C:2 * C]

    def remote(source, target, send, recv, device):
        return pltpu.make_async_remote_copy(
            src_ref=source, dst_ref=target, send_sem=send, recv_sem=recv,
            device_id=device, device_id_type=MESH)

    def sends(surf, sems, recvs, axis):
        return (
            remote(surf[axis].at[2], surf[axis].at[1], sems.at[0, axis], recvs.at[0, axis], mate_id),
            remote(surf[axis].at[2], surf[axis].at[3], sems.at[1, axis], recvs.at[1, axis], far_id),
        )

    fcopies = [sends(fsurf, fsend, frecv, axis) for axis in range(3)]
    hcopies = [sends(hsurf, hsend, hrecv, axis) for axis in range(3)]
    ecopies = [
        remote(fsurf[axis].at[2], esurf[axis].at[1], fsend.at[1, axis], frecv.at[1, axis], far_id)
        for axis in range(3)]
    pcopies = [
        remote(sums[axis], far_sums[axis], psend.at[axis], precv.at[axis], far_id) for axis in range(3)]
    tcopy = remote(nbr, ftab, psend.at[3], precv.at[3], far_id)

    order = (1, 0, 2)
    wcopies = [
        remote(wk1.at[i], mate1.at[i], wsend.at[n], wrecv.at[n], mate_id) for n, i in enumerate(order)]
    for n, i in enumerate(order):
        part = w2.at[core, pl.ds(9 * i, 9)]
        wcopies.append(remote(part, part, wsend.at[3 + n], wrecv.at[3 + n], mate_id))

    def prepare_faces():
        local[0].wait()
        for x in range(8):
            put(acc, slice(64 * x, 64 * x + 64), own[x].astype(F32))
        for axis in range(3):
            pack_pair(fsurf[axis].at[2], acc, lambda v: v.astype(BF16), axis)

    def prepare_own():
        for x in range(8):
            own_columns(cols.at[x], own[x])
        local[3].wait()
        for i in order:
            unpack(stage1, w1, core, i)

    def unpack_two():
        local[4].wait()
        for i in order:
            unpack(stage2, w2, core, i)

    def send_two():
        for n in range(3):
            wcopies[3 + n].start()

    def own_part(with_two=True, send=True):
        if with_two:
            local[4].wait()
        for n, i in enumerate(order):
            wcopies[n].wait_recv()
            unpack(mate1, w1, mate, i)
            if with_two:
                unpack(stage2, w2, core, i)
            for start, stop in (((1, 4), (4, 8)), ((0, 4), (4, 8)), ((0, 4), (4, 7)))[i]:
                rows = slice(64 * start, 64 * stop)
                d = own_product(cols, w1, i, start, stop)
                put(acc, rows, get(acc, rows) + d if n else d)
            if send:
                wcopies[3 + n].start()

    @pl.when(early)
    def _():
        prepare_faces()
        prepare_own()

    pl.when(first)(functools.partial(own_part, True, False))
    pl.semaphore_wait(barrier, 1 + has_far.astype(jnp.int32))

    @pl.when(jnp.logical_not(early))
    def _():
        for n in range(3):
            wcopies[n].start()
        prepare_faces()

    @pl.when(me == 1)
    def _():
        for n in range(3):
            wcopies[n].start()

    pl.when(long)(tcopy.start)
    for axis in range(3):
        pl.when(short)(fcopies[axis][1].start)
        pl.when(long)(ecopies[axis].start)
        fcopies[axis][0].start()

    @pl.when(early & (me != 1))
    def _():
        for n in range(3):
            wcopies[n].start()

    pl.when(jnp.logical_not(early))(prepare_own)

    local[1].wait()
    local[2].wait()
    where = []
    for t in range(27):
        n = tab[0, t]
        where.append(jnp.where(n < 0, 0, jnp.where(n == me, 2, jnp.where(n == mate_slot, 1, 3))))
    active = occs[0].astype(F32)

    pl.when(jnp.logical_not(first | second))(own_part)
    pl.when(second)(functools.partial(own_part, False, False))
    pl.when(first)(send_two)

    @pl.when(jnp.logical_not(long))
    def _():
        def arrived(axis):
            fcopies[axis][0].wait_recv()
            pl.when(short)(fcopies[axis][1].wait_recv)

        add_faces(acc, fcols, fsurf, where, w1, arrived)

    @pl.when(long)
    def _():
        near = [jnp.where(w == 3, 0, w) for w in where]
        add_faces(acc, fcols, fsurf, near, w1, lambda axis: fcopies[axis][0].wait_recv())
        for axis in range(3):
            pack_pair(sums[axis], acc, lambda v: v.astype(BF16), axis)
            pcopies[axis].start()

        @pl.when(second)
        def _():
            unpack_two()
            send_two()

        tcopy.wait_recv()
        fetch = pltpu.make_async_copy(ftab, tab2, lsem.at[5])
        fetch.start()
        facc[...] = jnp.zeros((2, 512, 128), F32)
        fetch.wait()
        given = [jnp.where(tab2[0, t] == me, 2, 0) for t in range(27)]
        add_faces(facc, fcols, fsurf, given, w1, lambda axis: None)
        for axis in range(3):
            pack_pair(given_sums[axis], facc, lambda v: v, axis)
        away = [jnp.where(w == 3, 1, 0) for w in where]
        add_faces(acc, fcols, esurf, away, w1, lambda axis: ecopies[axis].wait_recv())

    def hidden(v):
        return (jnp.maximum(v, 0.0) * active).astype(BF16)

    for axis in range(3):
        pack_pair(hsurf[axis].at[2], acc, hidden, axis)
        pl.when(short)(hcopies[axis][1].start)
        hcopies[axis][0].start()

    for n in range(3):
        wcopies[3 + n].wait_recv()
    for x in range(8):
        own_columns(cols.at[x], hidden(get(acc, slice(64 * x, 64 * x + 64))))
    res = own[0:4].reshape(256, C).astype(F32)
    d = own_product(cols, w2, 1, 0, 4) + own_product(cols, w2, 2, 0, 4) + res
    put(acc2, slice(0, 64), d[:64])
    put(acc2, slice(64, 256), d[64:] + own_product(cols, w2, 0, 1, 4))
    res = own[4:8].reshape(256, C).astype(F32)
    d = own_product(cols, w2, 1, 4, 8) + own_product(cols, w2, 0, 4, 8) + res
    put(acc2, slice(256, 448), d[:192] + own_product(cols, w2, 2, 4, 7))
    put(acc2, slice(448, 512), d[192:])
    act[...] = jnp.full((8, C), active, F32)

    for copy in wcopies:
        copy.wait_send()
    for axis in range(3):
        fcopies[axis][0].wait_send()
        pl.when(short)(fcopies[axis][1].wait_send)
        pl.when(long)(ecopies[axis].wait_send)

    @pl.when(long)
    def _():
        tcopy.wait_send()
        for axis in range(3):
            pcopies[axis].wait_send()

    def arrived(axis):
        hcopies[axis][0].wait_recv()
        pl.when(short)(hcopies[axis][1].wait_recv)

        @pl.when(long)
        def _():
            pcopies[axis].wait_recv()
            hsurf[axis][3] = jnp.maximum(
                far_sums[axis][...].astype(F32) + given_sums[axis][...], 0.0).astype(BF16)

    add_faces(acc2, fcols, hsurf, where, w2, arrived)
    for near, away in hcopies:
        near.wait_send()
        pl.when(short)(away.wait_send)


def finish_kernel(acc2, act, out, done, sem):
    scale = act[0:1, :]
    copies = []
    for part in range(4):
        for x in (2 * part, 2 * part + 1):
            done[x] = jnp.maximum(get(acc2, slice(64 * x, 64 * x + 64)), 0.0) * scale
        rows = pl.ds(2 * part, 2)
        copies.append(pltpu.make_async_copy(done.at[rows], out.at[rows], sem.at[part]))
        copies[part].start()
    for copy in copies:
        copy.wait()


def body(features, occupancy, neighbours, kernel_one, kernel_two):
    total = lax.axis_size("space") * lax.axis_size("wt")
    hbm = pl.BlockSpec(memory_space=pltpu.HBM)
    vmem = pl.BlockSpec(memory_space=pltpu.VMEM)

    def pinned(v):
        return pltpu.with_memory_space_constraint(v, pltpu.HBM)

    middle = pl.pallas_call(
        functools.partial(exchange_kernel, total),
        out_shape=(
            pltpu.VMEM((2, 512, 128), F32),
            pltpu.VMEM((8, C), F32),
        ),
        in_specs=[hbm] * 5,
        out_specs=(vmem,) * 2,
        scratch_shapes=[
            pltpu.VMEM((8, 64, C), BF16),
            *[pltpu.VMEM((4, 64, 2 * C), BF16)] * 3,
            *[pltpu.VMEM((2, 64, 2 * C), BF16)] * 3,
            *[pltpu.VMEM((4, 64, 2 * C), BF16)] * 3,
            *[pltpu.VMEM((3, 3, 3, 48, 2 * C), BF16)] * 3,
            pltpu.VMEM((2, 27, 96, C), BF16),
            pltpu.VMEM((2, 27, 96, C), BF16),
            pltpu.VMEM((8, 64, 9 * C), BF16),
            pltpu.VMEM((6, 64, 9 * C), BF16),
            pltpu.VMEM((2, 512, 128), F32),
            pltpu.VMEM((2, 512, 128), F32),
            *[pltpu.VMEM((64, 2 * C), BF16)] * 6,
            *[pltpu.VMEM((64, 2 * C), F32)] * 3,
            pltpu.VMEM((1, 27), jnp.int32),
            pltpu.SMEM((1, 27), jnp.int32),
            pltpu.SMEM((1, 27), jnp.int32),
            pltpu.SMEM((1,), jnp.int32),
            pltpu.SemaphoreType.DMA((6,)),
            pltpu.SemaphoreType.DMA((2, 3)),
            pltpu.SemaphoreType.DMA((2, 3)),
            pltpu.SemaphoreType.DMA((6,)),
            pltpu.SemaphoreType.DMA((6,)),
            pltpu.SemaphoreType.DMA((2, 3)),
            pltpu.SemaphoreType.DMA((2, 3)),
            pltpu.SemaphoreType.DMA((4,)),
            pltpu.SemaphoreType.DMA((4,)),
        ],
        compiler_params=pltpu.CompilerParams(
            collective_id=0, has_side_effects=True, vmem_limit_bytes=32 * 1024 * 1024),
    )(pinned(features.reshape(8, 64, C)), occupancy, pinned(neighbours), pinned(kernel_one), pinned(kernel_two))
    y = pl.pallas_call(
        finish_kernel,
        out_shape=jax.ShapeDtypeStruct((8, 64, C), F32),
        in_specs=[vmem] * 2,
        out_specs=hbm,
        scratch_shapes=[pltpu.VMEM((8, 64, C), F32), pltpu.SemaphoreType.DMA((4,))],
        compiler_params=pltpu.CompilerParams(vmem_limit_bytes=16 * 1024 * 1024),
    )(*middle)
    return y.reshape(1, 8, 8, 8, C)


def solution(mesh):
    return jax.shard_map(
        body,
        mesh=mesh,
        in_specs=(
            P(("space", "wt"), None, None, None, None),
            P(("space", "wt")),
            P(("space", "wt"), None),
            P(None, None, None, None, "wt"),
            P(None, None, None, None, "wt"),
        ),
        out_specs=P(("space", "wt"), None, None, None, None),
        check_vma=False,
    )
```
